32 devices in a mesh: exc: 2 (over x), slab: 16 (over z, y, core).
Axes of the slice: x: 2, y: 2, z: 4, core: 2. Of those that a mesh axis runs over, the one named last changes fastest.
Arguments:
- q_forward: float32 [2, 8192], P('exc', 'slab'), may hold values from -6 to 6
- q_adjoint: float32 [2, 8192], P('exc', 'slab'), may hold values from -6 to 6
- panel_offset: float32 [3, 8192], P(None, 'slab'), may hold values from -0.5 to 0.5
- block_anchor: int32 [3, 64], P(None, 'slab'), may hold values from 0 to 127, as said below
- kernel_hat: float32 [128, 128, 128], P(None, 'slab'), may hold values from 0.05 to 1, as said below
- near_list: int32 [64, 8], P('slab'), may hold values from 0 to 63, as said below
- near_count: int32 [64], P('slab'), may hold values from 1 to 8, as said below
- panel_vertices: int32 [3, 8192], P(None, 'slab'), may hold values from 0 to 1023, as said below
Outputs:
- vertex_grad: float32 [3, 1024], P(None, ('exc', 'slab'))
The draws below stay inside these ranges and needn't reach their ends.
Inputs may be any that keep to these rules, and one draw needn't show every extreme that they name: Block i lies in the planes of slab index i // 4: block_anchor[0, i] // 8 == i // 4. Even in every dimension: kernel_hat[a, b, c] equals kernel_hat[(-a) mod 128, (-b) mod 128, (-c) mod 128]. `near_list`: every entry of a block i's list, valid or not, is a block whose slab index differs from i // 4 by -1, 0 or 1 modulo the number of slab indices. `near_count`: some block has 8 valid entries. `panel_vertices`: vertex v belongs to slab index (v // 32) mod (number of slab indices); the vertices of a panel of block i belong to slab indices that differ from i // 4 by -1, 0 or 1 modulo the number of slab indices.
All inputs are finite; a program needn't handle non-finite values.
Results may differ from the reference program's by a relative error of at most 0.0003.
Values sent between devices are 32-bit elements; how exact they have to be, the bound alone decides.
No kernel may reach another device: no remote copies, remote signals or barrier semaphores. Data moves between devices by JAX's collectives and lax.ppermute only.
A program may use at most 256 MiB of HBM per device.

```python
import math
import jax
import jax.numpy as jnp
from jax import lax

G = 128
B = 128
NBD = 4
MAXN = 8
COND = 2
PL = 8
BLOCKS = 64
PANELS = 8192
VCH = 32
V = 1024
N_EXC = 2
N_SLAB = 16


def draw_block_anchor(key, part):
    keys = jax.random.split(jax.random.fold_in(key, 11), 3)
    owner = jnp.arange(BLOCKS, dtype=jnp.int32) // NBD
    plane = owner * PL + jax.random.randint(keys[0], (BLOCKS,), 0, PL, dtype=jnp.int32)
    row = (3 * owner + jax.random.randint(keys[1], (BLOCKS,), -3, 4, dtype=jnp.int32)) % G
    column = (2 * owner + jax.random.randint(keys[2], (BLOCKS,), -3, 4, dtype=jnp.int32)) % G
    return jnp.stack([plane, row, column]).astype(jnp.int32)


def draw_kernel_hat(key, part):
    inner = jax.random.fold_in(key, 13)
    base = jnp.exp(jax.random.uniform(inner, (G, G, G), jnp.float32, math.log(0.05), 0.0))
    mirror = jnp.roll(jnp.flip(base, (0, 1, 2)), 1, (0, 1, 2))
    return 0.5 * (base + mirror)


def draw_near_list(key, part):
    keys = jax.random.split(jax.random.fold_in(key, 17), 2)
    owner = jnp.arange(BLOCKS, dtype=jnp.int32) // NBD
    side = jax.random.randint(keys[0], (BLOCKS, MAXN), -1, 2, dtype=jnp.int32)
    local = jax.random.randint(keys[1], (BLOCKS, MAXN), 0, NBD, dtype=jnp.int32)
    return ((owner[:, None] + side) % N_SLAB * NBD + local).astype(jnp.int32)


def draw_near_count(key, part):
    counts = jax.random.randint(jax.random.fold_in(key, 19), (BLOCKS,), 1, MAXN + 1, dtype=jnp.int32)
    return counts.at[0].set(MAXN)


def draw_panel_vertices(key, part):
    keys = jax.random.split(jax.random.fold_in(key, 23), 3)
    owner = jnp.arange(PANELS, dtype=jnp.int32) // (NBD * B)
    side = jax.random.randint(keys[0], (3, PANELS), -1, 2, dtype=jnp.int32)
    slab_owner = (owner[None, :] + side) % N_SLAB
    part_index = jax.random.randint(keys[1], (3, PANELS), 0, N_EXC, dtype=jnp.int32)
    place = jax.random.randint(keys[2], (3, PANELS), 0, VCH, dtype=jnp.int32)
    return ((part_index * N_SLAB + slab_owner) * VCH + place).astype(jnp.int32)


def block_scale(rng, shape, cuts, least, top_value):
    def one(dim, blocks):
        draws = jax.random.uniform(jax.random.fold_in(jax.random.fold_in(rng, 6), dim), (blocks,), jnp.float32, least / len(cuts), top_value / len(cuts))
        return jnp.repeat(jnp.exp(draws), shape[dim] // blocks).reshape((-1,) + (1,) * (len(shape) - dim - 1))

    level = one(*cuts[0])
    for cut in cuts[1:]:
        level = level * one(*cut)
    return level


def centred(own_key, dims, deviation, most, cuts=(), kind=jnp.bfloat16):
    loudness = block_scale(own_key, dims, cuts, -0.22, 0.18) if cuts else 1.0
    result = jax.random.normal(own_key, dims, jnp.float32) * deviation * loudness
    return jnp.minimum(jnp.maximum(result, -most), most).astype(kind)


def setup_inputs(seed: int = 0) -> dict:
    arg_keys = jax.random.split(jax.random.key(seed), 9)
    return {
        "q_forward": centred(arg_keys[0], (COND, PANELS), 1.0, 6.0, ((0, 2), (1, 16)), jnp.float32),
        "q_adjoint": centred(arg_keys[1], (COND, PANELS), 1.0, 6.0, ((0, 2), (1, 16)), jnp.float32),
        "panel_offset": jnp.clip(jax.random.uniform(arg_keys[2], (3, PANELS), jnp.float32, -0.5, 0.5) * block_scale(arg_keys[2], (3, PANELS), ((1, 16),), -0.4, 0.0), -0.5, 0.5),
        "block_anchor": draw_block_anchor(jax.random.fold_in(arg_keys[8], 71), 0),
        "kernel_hat": draw_kernel_hat(jax.random.fold_in(arg_keys[8], 71), 0),
        "near_list": draw_near_list(jax.random.fold_in(arg_keys[8], 71), 0),
        "near_count": draw_near_count(jax.random.fold_in(arg_keys[8], 71), 0),
        "panel_vertices": draw_panel_vertices(jax.random.fold_in(arg_keys[8], 71), 0),
    }


soften_sq = 16.0
highest = lax.Precision.HIGHEST

def lagrange(offset):
    values = jnp.stack([0.5 * offset * (offset - 1.0), 1.0 - offset * offset, 0.5 * offset * (offset + 1.0)])
    slopes = jnp.stack([offset - 0.5, -2.0 * offset, offset + 0.5])
    return (values, slopes)

def stencil_index(plane, row, column, length, plane_count):
    shifts = jnp.arange(3, dtype=jnp.int32) - 1
    planes = (plane[:, None] + shifts[None, :]) % plane_count
    rows = (row[:, None] + shifts[None, :]) % length
    columns = (column[:, None] + shifts[None, :]) % length
    flat = planes[:, :, None, None] * (length * length) + rows[:, None, :, None] * length + columns[:, None, None, :]
    return flat.reshape(plane.shape[0], 27).astype(jnp.int32)

def block_charges(charges, values):
    return jnp.einsum('fbp,ibp,jbp,kbp->fbijk', charges, values[:, 0], values[:, 1], values[:, 2], precision=highest)

def far_gradient(potential, charges, values, slopes):
    first = jnp.einsum('fbijk,ibp,jbp,kbp->fbp', potential, slopes[:, 0], values[:, 1], values[:, 2], precision=highest)
    second = jnp.einsum('fbijk,ibp,jbp,kbp->fbp', potential, values[:, 0], slopes[:, 1], values[:, 2], precision=highest)
    third = jnp.einsum('fbijk,ibp,jbp,kbp->fbp', potential, values[:, 0], values[:, 1], slopes[:, 2], precision=highest)
    parts = jnp.stack([first, second, third])
    return parts[:, 0] * charges[1][None] + parts[:, 1] * charges[0][None]

def near_gradient(position, forward, adjoint, near_list, near_count):
    mask = (jnp.arange(MAXN, dtype=jnp.int32)[None, :] < near_count[:, None]).astype(jnp.float32)
    groups = BLOCKS // NBD

    def per_group(group):
        rows = (group * NBD + jnp.arange(NBD, dtype=jnp.int32)).astype(jnp.int32)
        own_position = position[:, rows]
        own_forward = forward[:, rows]
        own_adjoint = adjoint[:, rows]
        total = jnp.zeros((3, NBD, B), jnp.float32)
        for slot in range(MAXN):
            other = near_list[rows, slot]
            other_position = position[:, other]
            diff = own_position[:, :, :, None] - other_position[:, :, None, :]
            inverse = lax.rsqrt(lax.optimization_barrier(jnp.sum(diff * diff, axis=0)) + soften_sq)
            pair = jnp.einsum('nbp,nbr->bpr', own_adjoint, forward[:, other], precision=highest)
            pair = pair + jnp.einsum('nbp,nbr->bpr', own_forward, adjoint[:, other], precision=highest)
            weight = pair * inverse * inverse * inverse
            total = total - mask[rows, slot][None, :, None] * lax.optimization_barrier(jnp.sum(diff * weight[None], axis=3))
        return total
    stacked = lax.map(per_group, jnp.arange(groups, dtype=jnp.int32))
    return jnp.transpose(stacked, (1, 0, 2, 3)).reshape(3, BLOCKS, B)

def reference(q_forward, q_adjoint, panel_offset, block_anchor, kernel_hat, near_list, near_count, panel_vertices):
    offset = panel_offset.reshape(3, BLOCKS, B)
    values, slopes = lagrange(offset)
    flat = stencil_index(block_anchor[0], block_anchor[1], block_anchor[2], G, G)
    far_total = jnp.zeros((3, BLOCKS, B), jnp.float32)
    for conductor in range(COND):
        charges = jnp.stack([q_forward[conductor], q_adjoint[conductor]]).reshape(2, BLOCKS, B)
        spread = block_charges(charges, values).reshape(2, -1)
        grid = jnp.zeros((2, G * G * G), jnp.float32).at[:, flat.reshape(-1)].add(spread).reshape(2, G, G, G)
        spectrum = jnp.fft.fftn(grid, axes=(1, 2, 3)) * kernel_hat[None]
        potential = jnp.real(jnp.fft.ifftn(spectrum, axes=(1, 2, 3))).astype(jnp.float32)
        stencil_values = potential.reshape(2, -1)[:, flat].reshape(2, BLOCKS, 3, 3, 3)
        far_total = far_total + far_gradient(stencil_values, charges, values, slopes)
    position = offset + block_anchor.astype(jnp.float32)[:, :, None]
    forward = q_forward.reshape(COND, BLOCKS, B)
    adjoint = q_adjoint.reshape(COND, BLOCKS, B)
    near_total = near_gradient(position, forward, adjoint, near_list, near_count)
    panel_grad = ((far_total + near_total) / (3.0 * COND)).reshape(3, PANELS)
    vertex_grad = jnp.zeros((3, V), jnp.float32)
    for corner in range(3):
        vertex_grad = vertex_grad.at[:, panel_vertices[corner]].add(panel_grad)
    return vertex_grad
```

```python
import functools
import math

import jax
import jax.numpy as jnp
import numpy as np
from jax import lax
from jax.experimental import pallas as pl
from jax.experimental.pallas import tpu as pltpu
from jax.sharding import PartitionSpec as P

VCH = 32
QROWS = 9
soften_sq = 16.0
highest = lax.Precision.HIGHEST
VM = pl.BlockSpec(memory_space=pltpu.VMEM)
SM = pl.BlockSpec(memory_space=pltpu.SMEM)


def mm(a, b):
    return lax.dot_general(
        a, b, (((1,), (0,)), ((), ())), precision=highest, preferred_element_type=jnp.float32
    )


def mm_nt(a, b):
    return lax.dot_general(
        a, b, (((1,), (1,)), ((), ())), precision=highest, preferred_element_type=jnp.float32
    )


def iota(shape, dim):
    return lax.broadcasted_iota(jnp.int32, shape, dim)


@functools.lru_cache(None)
def tables(g, thick):
    n = np.arange(g)
    ang = 2.0 * np.pi * (np.outer(n, n) % g) / g
    cos, sin = np.cos(ang), np.sin(ang)
    th = 2.0 * np.pi * n / g
    u = np.stack([np.ones(g), -1j * np.sin(th), np.cos(th) - 1.0])
    half = g // 2
    e = u[:, :, None] * (cos - 1j * sin)[None]
    rows = np.concatenate([e.real[:, : half + 1], -e.imag[:, 1:half]], axis=1)
    ct = np.concatenate([rows[k].T for k in range(3)], axis=1)
    cz = np.concatenate([cos, sin], axis=1)
    nb3 = 3 * thick
    up = np.zeros((2 * nb3, 2 * g))
    dn = np.zeros((2 * g, 2 * nb3))
    for b in range(thick):
        for k in range(3):
            r, i = b * 3 + k, nb3 + b * 3 + k
            up[r, :g], up[r, g:] = u[k].real, u[k].imag
            up[i, :g], up[i, g:] = -u[k].imag, u[k].real
            uc = np.conj(u[k])
            dn[:g, r], dn[g:, r] = uc.real, -uc.imag
            dn[:g, i], dn[g:, i] = uc.imag, uc.real
    m = np.zeros((2, 3, 128, 2 * nb3))
    bt = np.zeros((2, 3, 2 * nb3, 128))
    for b in range(thick):
        for k in range(3):
            r, i = b * 3 + k, nb3 + b * 3 + k
            for al in range(3):
                f0, f1 = al * 9 + k, 27 + al * 9 + k
                m[0, 0, f0, r] = 1
                m[0, 0, f1, i] = 1
                m[0, 1, f0 + 3, i] = -1
                m[0, 1, f1 + 3, r] = 1
                m[0, 2, f0 + 6, r] = 1
                m[0, 2, f1 + 6, i] = 1
            bt[0, 0, r, k] = 1
            bt[0, 0, i, 9 + k] = 1
            bt[0, 1, r, 9 + 3 + k] = 1
            bt[0, 1, i, 3 + k] = -1
            bt[0, 2, r, 6 + k] = 1
            bt[0, 2, i, 9 + 6 + k] = 1
    m[1, :, :, :nb3], m[1, :, :, nb3:] = m[0, :, :, nb3:], -m[0, :, :, :nb3]
    bt[1, :, :nb3], bt[1, :, nb3:] = bt[0, :, nb3:], -bt[0, :, :nb3]
    bt = bt / float(g) ** 3
    lanes = np.zeros((1, 2 * nb3))
    lanes[0] = np.tile(np.arange(thick).repeat(3), 2)
    bt = bt.transpose(0, 1, 3, 2)
    return [x.astype(np.float32) for x in (ct, cz, up, dn, m, bt[:, :, :32], lanes)]


def pack_kernel(slabs, blocks, qf, qa, off, anchor, verts, out, buf):
    width = qf.shape[1] // blocks
    buf[...] = jnp.zeros_like(buf)
    for l in range(blocks):
        cut = slice(l * width, (l + 1) * width)
        buf[blocks + l : blocks + l + 1, :] = qf[:, cut]
        buf[2 * blocks + l : 2 * blocks + l + 1, :] = qa[:, cut]
        for c in range(3):
            row = (3 + c) * blocks + l
            buf[row : row + 1, :] = off[c : c + 1, cut]
            row = (6 + c) * blocks + l
            buf[row : row + 1, :] = verts[c : c + 1, cut].astype(jnp.float32)
    part = lambda q: buf[q * blocks : (q + 1) * blocks, :]
    t0, t1, t2 = part(3), part(4), part(5)
    lane = iota((blocks, 128), 1)
    sub = iota((blocks, 128), 0)
    acc = jnp.zeros((blocks, 128), jnp.float32)
    for f in range(2):
        x = part(1 + f)
        for al in range(3):
            y = x
            for be in range(3):
                z = y
                for ga in range(3):
                    idx = f * 27 + al * 9 + be * 3 + ga
                    acc = jnp.where(lane == idx, jnp.sum(z, axis=1, keepdims=True), acc)
                    z = z * t2
                y = y * t1
            x = x * t0
    for l in range(blocks):
        for c in range(3):
            hit = (lane == 54 + c) & (sub == l)
            acc = jnp.where(hit, anchor[c, l].astype(jnp.float32), acc)
    buf[0:blocks, :] = acc
    whole = buf[...]
    for j in range(slabs):
        out[j] = whole


def prep_kernel(k, ka, kd):
    g = k.shape[0]
    half = g // 2
    for a in range(half):
        if a == 0:
            top, bot, dif = k[0], k[half], jnp.zeros_like(k[0])
        else:
            top = k[a] + k[g - a]
            bot, dif = top, k[a] - k[g - a]
        ka[:, a, :] = top
        ka[:, half + a, :] = bot
        kd[:, a, :] = dif


def main_kernel(
    slabs, exc, blocks, thick, g,
    slab_ref, near_list, near_count,
    gat, ka, kd, ct_t, cz_t, up_t, dn_t, m_t, bt_t, lane_t,
    out, qs, rr, grad, own, acc,
):
    nblk = slabs * blocks
    half = g // 2
    nb3 = 3 * thick
    slab = slab_ref[0]
    for s in range(slabs):
        for q in range(QROWS):
            qs[q, s * blocks : (s + 1) * blocks, :] = gat[s, q * blocks : (q + 1) * blocks, :]
    head = qs[0]
    lane = iota((nblk, 128), 1)
    xcol, ycol, zcol = (head[:, 54 + c : 55 + c].astype(jnp.int32) for c in range(3))
    glane = iota((nblk, g), 1)
    hot = lambda col: jnp.where(glane == col, 1.0, 0.0)
    ct = mm(hot(xcol), ct_t[...])
    ct = jnp.concatenate([ct[:, k * g : (k + 1) * g] for k in range(3)], axis=0)
    cc = jnp.transpose(ct)
    wz = mm(hot(zcol), cz_t[...])
    wc = jnp.concatenate([wz[:, :g]] * 3, axis=0)
    ws = jnp.concatenate([wz[:, g:]] * 3, axis=0)
    freq = lane_t[...].astype(jnp.int32) + slab * thick
    step = 2.0 * math.pi / g
    th = freq.astype(jnp.float32) * step
    sn, cm = jnp.sin(th), jnp.cos(th) - 1.0
    turn = ((ycol * freq) & (g - 1)).astype(jnp.float32) * step
    pc, ps = jnp.cos(turn), jnp.sin(turn)
    m0 = m_t[0, 0] + m_t[0, 1] * sn + m_t[0, 2] * cm
    m1 = m_t[1, 0] + m_t[1, 1] * sn + m_t[1, 2] * cm
    vs = []
    for al in range(3):
        lo, hi = al * 9, al * 9 + 9
        keep = ((lane >= lo) & (lane < hi)) | ((lane >= 27 + lo) & (lane < 27 + hi))
        qa_ = jnp.where(keep, head, 0.0)
        vs.append(mm(qa_, m0) * pc + mm(qa_, m1) * ps)
    v = jnp.concatenate(vs, axis=0)
    vlane = lane_t[...].astype(jnp.int32)
    x = jnp.zeros((3 * nblk, 2 * nb3), jnp.float32)
    for b in range(thick):
        a = mm(jnp.where(vlane == b, v, 0.0), up_t[...])
        ar, ai = a[:, :g], a[:, g:]
        r = jnp.concatenate([ar * wc + ai * ws, ai * wc - ar * ws], axis=1)
        pn = mm(cc, r)
        pr, pi = pn[:half, :g], pn[:half, g:]
        nr, ni = pn[half:, :g], pn[half:, g:]
        kt, kb, kx = ka[b, :half, :], ka[b, half:, :], kd[b]
        top = jnp.concatenate([pr * kt + ni * kx, pi * kt - nr * kx], axis=1)
        bot = jnp.concatenate([nr * kb - pi * kx, ni * kb + pr * kx], axis=1)
        z = mm(ct, jnp.concatenate([top, bot], axis=0))
        zr, zi = z[:, :g], z[:, g:]
        y = jnp.concatenate([zr * wc - zi * ws, zi * wc + zr * ws], axis=1)
        x = jnp.where(vlane == b, mm(y, dn_t[...]), x)
    b0 = bt_t[0, 0] + bt_t[0, 1] * sn + bt_t[0, 2] * cm
    b1 = bt_t[1, 0] + bt_t[1, 1] * sn + bt_t[1, 2] * cm
    pcs = jnp.concatenate([pc] * 3, axis=0)
    pss = jnp.concatenate([ps] * 3, axis=0)
    coef = mm_nt(x * pcs, b0) + mm_nt(x * pss, b1)
    qf, qa, t0, t1, t2 = (qs[k] for k in range(1, 6))
    va, vb, vc = [], [], []
    for al in range(3):
        rows = coef[al * nblk : (al + 1) * nblk]
        mid = []
        for be in range(3):
            h = []
            for ga in range(3):
                k = be * 3 + ga
                h.append(qa * rows[:, k : k + 1] + qf * rows[:, 9 + k : 10 + k])
            mid.append((h[0] + t2 * (h[1] + t2 * h[2]), h[1] + 2.0 * t2 * h[2]))
        va.append(mid[0][0] + t1 * (mid[1][0] + t1 * mid[2][0]))
        vb.append(mid[1][0] + 2.0 * t1 * mid[2][0])
        vc.append(mid[0][1] + t1 * (mid[1][1] + t1 * mid[2][1]))
    grad[0] = va[1] + 2.0 * t0 * va[2]
    grad[1] = vb[0] + t0 * (vb[1] + t0 * vb[2])
    grad[2] = vc[0] + t0 * (vc[1] + t0 * vc[2])
    base = slab * blocks
    own[...] = jnp.zeros_like(own)
    for q in range(5):
        own[q * blocks : (q + 1) * blocks, :] = qs[1 + q, pl.ds(base, blocks), :]
    cols = jnp.transpose(own[...])
    for l in range(blocks):
        pick = lambda q: cols[:, q * blocks + l : q * blocks + l + 1]
        xi = [pick(2 + c) for c in range(3)]
        me = qs[0, pl.ds(base + l, 1), :]
        rr[...] = jnp.zeros_like(rr)
        for slot in range(near_list.shape[1]):

            @pl.when(slot < near_count[l])
            def _():
                src = near_list[l, slot]
                away = qs[0, pl.ds(src, 1), :] - me
                fr, ad = qs[1, pl.ds(src, 1), :], qs[2, pl.ds(src, 1), :]
                xr = [qs[3 + c, pl.ds(src, 1), :] + away[:, 54 + c : 55 + c] for c in range(3)]
                d = [xi[c] - xr[c] for c in range(3)]
                inv = lax.rsqrt(d[0] * d[0] + d[1] * d[1] + d[2] * d[2] + soften_sq)
                cube = inv * inv * inv
                right = [fr] + [fr * xr[c] for c in range(3)] + [ad] + [ad * xr[c] for c in range(3)]
                rr[...] += mm_nt(cube, jnp.concatenate(right, axis=0))

        o = rr[...]
        fi, di = pick(0), pick(1)
        res = []
        for c in range(3):
            res.append(
                -di * (xi[c] * o[:, 0:1] - o[:, 1 + c : 2 + c])
                - fi * (xi[c] * o[:, 4:5] - o[:, 5 + c : 6 + c])
            )
        wide = jnp.concatenate([jnp.broadcast_to(r, (r.shape[0], 8)) for r in res], axis=1)
        back = jnp.transpose(wide)
        for c in range(3):
            grad[c, pl.ds(base + l, 1), :] += back[8 * c : 8 * c + 1, :]
    acc[...] = jnp.zeros_like(acc)
    wrow = (3 * exc + 7) // 8 * 8
    scale = 1.0 / (3.0 * exc)
    hrow = iota((wrow, 128), 0)
    lrow = iota((VCH, 128), 0)
    for s in range(slabs):
        left, right = [], []
        for l in range(blocks):
            row = s * blocks + l
            gs = [grad[c, row : row + 1, :] * scale for c in range(3)]
            for k in range(3):
                vert = qs[6 + k, row : row + 1, :].astype(jnp.int32)
                chunk, place = vert // VCH, vert % VCH
                rel = (chunk % slabs - s + 1 + slabs) % slabs
                hit = hrow == chunk // slabs * 3 + rel
                left.append(jnp.concatenate([jnp.where(hit, gs[c], 0.0) for c in range(3)], axis=0))
                right.append(jnp.where(lrow == place, 1.0, 0.0))
        tot = mm_nt(jnp.concatenate(left, axis=1), jnp.concatenate(right, axis=1))
        for c in range(3):
            for e in range(exc):
                acc[c, e, s : s + 3, 0:VCH] += tot[c * wrow + e * 3 : c * wrow + e * 3 + 3, :]
    for e in range(exc):
        sums = []
        for c in range(3):
            acc[c, e, 1:2, :] += acc[c, e, slabs + 1 : slabs + 2, :]
            acc[c, e, slabs : slabs + 1, :] += acc[c, e, 0:1, :]
            sums.append(acc[c, e, 1 : slabs + 1, :])
        out[e * slabs : (e + 1) * slabs, :] = (
            sums[0] + pltpu.roll(sums[1], VCH, 1) + pltpu.roll(sums[2], 2 * VCH, 1)
        )


def sum_kernel(parts, out):
    row = jnp.sum(parts[...], axis=0, keepdims=True)
    for c in range(3):
        out[c : c + 1, :] = row[:, c * VCH : (c + 1) * VCH]


def on_device(
    q_forward, q_adjoint, panel_offset, block_anchor, kernel_hat, near_list, near_count,
    panel_vertices,
):
    slabs, exc = lax.axis_size("slab"), lax.axis_size("exc")
    blocks = block_anchor.shape[1]
    g, thick = kernel_hat.shape[0], kernel_hat.shape[1]
    nblk = slabs * blocks
    f32 = jnp.float32
    shape = lambda *s: jax.ShapeDtypeStruct(s, f32)
    rows = QROWS * blocks
    packed = pl.pallas_call(
        functools.partial(pack_kernel, slabs, blocks),
        out_shape=shape(slabs, rows, 128),
        in_specs=[VM, VM, VM, SM, VM],
        out_specs=VM,
        scratch_shapes=[pltpu.VMEM((rows, 128), f32)],
        name="pack",
    )(q_forward, q_adjoint, panel_offset, block_anchor, panel_vertices)
    ka, kd = pl.pallas_call(
        prep_kernel,
        out_shape=(shape(thick, g, g), shape(thick, g // 2, g)),
        in_specs=[VM],
        out_specs=(VM, VM),
        name="prep",
    )(kernel_hat)
    gathered = lax.all_to_all(packed, "slab", split_axis=0, concat_axis=0, tiled=True)
    consts = tables(g, thick)
    slab = lax.axis_index("slab").astype(jnp.int32).reshape(1)
    partial = pl.pallas_call(
        functools.partial(main_kernel, slabs, exc, blocks, thick, g),
        out_shape=shape(exc * slabs, 128),
        in_specs=[SM] * 3 + [VM] * (3 + len(consts)),
        out_specs=VM,
        scratch_shapes=[
            pltpu.VMEM((QROWS, nblk, 128), f32),
            pltpu.VMEM((128, 8), f32),
            pltpu.VMEM((3, nblk, 128), f32),
            pltpu.VMEM((-(-5 * blocks // 128) * 128, 128), f32),
            pltpu.VMEM((3, exc, slabs + 2, 128), f32),
        ],
        name="field",
    )(slab, near_list, near_count, gathered, ka, kd, *[jnp.asarray(c) for c in consts])
    parts = lax.all_to_all(partial, ("exc", "slab"), split_axis=0, concat_axis=0, tiled=True)
    return pl.pallas_call(
        sum_kernel, out_shape=shape(3, VCH), in_specs=[VM], out_specs=VM, name="total"
    )(parts)


def solution(mesh):
    return jax.shard_map(
        on_device,
        mesh=mesh,
        in_specs=(
            P("exc", "slab"),
            P("exc", "slab"),
            P(None, "slab"),
            P(None, "slab"),
            P(None, "slab", None),
            P("slab", None),
            P("slab"),
            P(None, "slab"),
        ),
        out_specs=P(None, ("exc", "slab")),
        check_vma=False,
    )
```

```python
import functools
import math

import jax
import jax.numpy as jnp
import numpy as np
from jax import lax
from jax.experimental import pallas as pl
from jax.experimental.pallas import tpu as pltpu
from jax.sharding import PartitionSpec as P

VCH = 32
QROWS = 9
soften_sq = 16.0
bf16 = jnp.bfloat16
f32 = jnp.float32
VM = pl.BlockSpec(memory_space=pltpu.VMEM)
SM = pl.BlockSpec(memory_space=pltpu.SMEM)
LIMIT = 24 << 20


def split(x):
    high = x.astype(bf16)
    return high, (x - high.astype(f32)).astype(bf16)


def mm(a, b):
    return lax.dot_general(a, b, (((1,), (0,)), ((), ())), preferred_element_type=f32)


def mm_nt(a, b):
    return lax.dot_general(a, b, (((1,), (1,)), ((), ())), preferred_element_type=f32)


def beside(*parts):
    return jnp.concatenate(parts, axis=1)


def below(*parts):
    return jnp.concatenate(parts, axis=0)


def iota(shape, dim):
    return lax.broadcasted_iota(jnp.int32, shape, dim)


@functools.lru_cache(None)
def tables(g, thick):
    n = np.arange(g)
    ang = 2.0 * np.pi * (np.outer(n, n) % g) / g
    cos, sin = np.cos(ang), np.sin(ang)
    th = 2.0 * np.pi * n / g
    u = np.stack([np.ones(g), -1j * np.sin(th), np.cos(th) - 1.0])
    half = g // 2
    e = u[:, :, None] * (cos - 1j * sin)[None]
    rows = np.concatenate([e.real[:, : half + 1], -e.imag[:, 1:half]], axis=1)
    ct = np.concatenate([rows[k].T for k in range(3)], axis=1)
    cz = np.concatenate([cos, sin], axis=1)
    nb3 = 3 * thick
    up = np.zeros((64, 2 * g))
    dn = np.zeros((2 * g, 64))
    m = np.zeros((2, 3, 128, 64))
    bt = np.zeros((2, 3, 64, 128))
    for b in range(thick):
        for k in range(3):
            r, i = b * 3 + k, nb3 + b * 3 + k
            up[r, :g], up[r, g:] = u[k].real, u[k].imag
            up[i, :g], up[i, g:] = -u[k].imag, u[k].real
            uc = np.conj(u[k])
            dn[:g, r], dn[g:, r] = uc.real, -uc.imag
            dn[:g, i], dn[g:, i] = uc.imag, uc.real
            for al in range(3):
                f0, f1 = al * 9 + k, 27 + al * 9 + k
                m[0, 0, f0, r] = 1
                m[0, 0, f1, i] = 1
                m[0, 1, f0 + 3, i] = -1
                m[0, 1, f1 + 3, r] = 1
                m[0, 2, f0 + 6, r] = 1
                m[0, 2, f1 + 6, i] = 1
            bt[0, 0, r, k] = 1
            bt[0, 0, i, 9 + k] = 1
            bt[0, 1, r, 9 + 3 + k] = 1
            bt[0, 1, i, 3 + k] = -1
            bt[0, 2, r, 6 + k] = 1
            bt[0, 2, i, 9 + 6 + k] = 1
    real, imag = slice(0, nb3), slice(nb3, 2 * nb3)
    m[1, ..., real], m[1, ..., imag] = m[0, ..., imag], -m[0, ..., real]
    bt[1, :, real], bt[1, :, imag] = bt[0, :, imag], -bt[0, :, real]
    bt = bt / float(g) ** 3
    m = np.concatenate([m, m], axis=3)
    bt = np.concatenate([bt, bt], axis=2)
    lanes = np.full((64,), -1)
    lanes[: 2 * nb3] = np.tile(np.arange(thick).repeat(3), 2)
    lanes = np.tile(lanes, 2)[None]

    def halves(x):
        high = x.astype(np.float32).astype(bf16)
        return high, (x.astype(np.float32) - high.astype(np.float32)).astype(bf16)

    ct_h, ct_l = halves(ct)
    cz_h, cz_l = halves(cz)
    up_h, up_l = halves(up)
    dn_h, dn_l = halves(dn)
    up4 = np.concatenate([up_h, up_h, up_l, np.zeros_like(up_l)], axis=0)
    dn2 = np.concatenate([np.concatenate([dn_h, dn_l], axis=1)] * 2, axis=0)
    ctz = np.concatenate([ct_h, ct_l], axis=1)
    czz = np.concatenate([cz_h, cz_l], axis=1)
    return (ctz, czz, up4, dn2), (m.astype(np.float32), bt.astype(np.float32)), lanes.astype(np.int32)


def pack_kernel(slabs, blocks, qf, qa, off, anchor, verts, out, buf):
    width = qf.shape[1] // blocks
    buf[...] = jnp.zeros_like(buf)
    for l in range(blocks):
        cut = slice(l * width, (l + 1) * width)
        buf[blocks + l : blocks + l + 1, :] = qf[:, cut]
        buf[2 * blocks + l : 2 * blocks + l + 1, :] = qa[:, cut]
        for c in range(3):
            row = (3 + c) * blocks + l
            buf[row : row + 1, :] = off[c : c + 1, cut]
            row = (6 + c) * blocks + l
            buf[row : row + 1, :] = verts[c : c + 1, cut].astype(f32)
    part = lambda q: buf[q * blocks : (q + 1) * blocks, :]
    t0, t1, t2 = part(3), part(4), part(5)
    lane = iota((blocks, 128), 1)
    sub = iota((blocks, 128), 0)
    acc = jnp.zeros((blocks, 128), f32)
    for f in range(2):
        x = part(1 + f)
        for al in range(3):
            y = x
            for be in range(3):
                z = y
                for ga in range(3):
                    idx = f * 27 + al * 9 + be * 3 + ga
                    acc = jnp.where(lane == idx, jnp.sum(z, axis=1, keepdims=True), acc)
                    z = z * t2
                y = y * t1
            x = x * t0
    for l in range(blocks):
        for c in range(3):
            hit = (lane == 54 + c) & (sub == l)
            acc = jnp.where(hit, anchor[c, l].astype(f32), acc)
    buf[0:blocks, :] = acc
    whole = buf[...]
    for j in range(slabs):
        out[j] = whole


def prep_kernel(thick, slab_ref, k, m_t, bt_t, lane_t, ka, kd, mo, bo, fy):
    g = k.shape[0]
    half = g // 2
    for a in range(half):
        if a == 0:
            top, bot, dif = k[0], k[half], jnp.zeros_like(k[0])
        else:
            top = k[a] + k[g - a]
            bot, dif = top, k[a] - k[g - a]
        ka[:, a, :] = top
        ka[:, half + a, :] = bot
        kd[:, a, :] = dif
    freq = lane_t[...] + slab_ref[0] * thick
    step = 2.0 * math.pi / g
    th = freq.astype(f32) * step
    sn, cm = jnp.sin(th), jnp.cos(th) - 1.0
    for v in range(2):
        h, l = split(m_t[v, 0] + m_t[v, 1] * sn + m_t[v, 2] * cm)
        mo[v] = below(h, h, l)
    pieces = []
    for v in range(2):
        h, l = split(bt_t[v, 0] + bt_t[v, 1] * jnp.transpose(jnp.broadcast_to(sn, (128, 128)))
                     + bt_t[v, 2] * jnp.transpose(jnp.broadcast_to(cm, (128, 128))))
        pieces += [h, h, l]
    bo[...] = below(*pieces)
    turn = ((iota((g, 128), 0) * freq) & (g - 1)).astype(f32) * step
    ch, cl = split(jnp.cos(turn))
    sh, sl = split(jnp.sin(turn))
    fy[...] = beside(ch, sh, cl, sl)


def main_kernel(
    slabs, exc, blocks, thick, g,
    slots, facts_any,
    gat, ka, kd, mo, bo, fy, ct_t, cz_t, up_t, dn_t, lane_t,
    out, qs, grad, expand, reduced, facts, sem,
):
    copy = pltpu.make_async_copy(facts_any, facts, sem)
    copy.start()
    nblk = slabs * blocks
    half = g // 2
    for s in range(slabs):
        for q in range(QROWS):
            qs[q, s * blocks : (s + 1) * blocks, :] = gat[s, q * blocks : (q + 1) * blocks, :]
    head = qs[0]
    lane = iota((nblk, 128), 1)
    glane = iota((nblk, g), 1).astype(f32)
    hot = lambda c: jnp.where(glane == head[:, 54 + c : 55 + c], 1.0, 0.0).astype(bf16)
    cth = mm(hot(0), ct_t[...])
    rows3 = lambda x, o: below(*[x[:, o + k * g : o + (k + 1) * g] for k in range(3)])
    ct_h, ct_l = rows3(cth, 0), rows3(cth, 3 * g)
    cc_h = jnp.transpose(ct_h).astype(bf16)
    cc = below(cc_h, jnp.transpose(ct_l).astype(bf16))
    ct_h, ct_l = ct_h.astype(bf16), ct_l.astype(bf16)
    ct = below(beside(ct_h, ct_h), beside(ct_l, jnp.zeros_like(ct_l)))
    wz = mm(hot(2), cz_t[...])
    wz = wz[:, : 2 * g] + wz[:, 2 * g :]
    wc = below(*[wz[:, :g]] * 3)
    ws = below(*[wz[:, g:]] * 3)
    ph = mm(hot(1), fy[...])
    ph = ph[:, :256] + ph[:, 256:]
    pc, ps = ph[:, :128], ph[:, 128:]
    vs = []
    for al in range(3):
        lo, hi = al * 9, al * 9 + 9
        keep = ((lane >= lo) & (lane < hi)) | ((lane >= 27 + lo) & (lane < 27 + hi))
        h, l = split(jnp.where(keep, head, 0.0))
        q3 = beside(h, l, h)
        vs.append(mm(q3, mo[0]) * pc + mm(q3, mo[1]) * ps)
    v = below(*vs)
    vh = v.astype(bf16).astype(f32)
    v = jnp.where(iota(v.shape, 1) < 64, vh, v - vh)
    vlane = lane_t[...]
    m3 = 3 * nblk
    vb = below(*[jnp.where(vlane == b, v, 0.0) for b in range(thick)]).astype(bf16)
    expand[...] = mm(beside(vb, vb), up_t[...])
    for b in range(thick):
        ar, ai = expand[b * m3 : (b + 1) * m3, :g], expand[b * m3 : (b + 1) * m3, g:]
        rh, rl = split(beside(ar * wc + ai * ws, ai * wc - ar * ws))
        pn = mm(cc, rh)
        pn = pn[:g] + pn[g:] + mm(cc_h, rl)
        pr, pi = pn[:half, :g], pn[:half, g:]
        nr, ni = pn[half:, :g], pn[half:, g:]
        kt, kb, kx = ka[b, :half, :], ka[b, half:, :], kd[b]
        top = beside(pr * kt + ni * kx, pi * kt - nr * kx)
        bot = beside(nr * kb - pi * kx, ni * kb + pr * kx)
        th, tl = split(below(top, bot))
        z = mm(ct, below(th, tl))
        z = z[:m3] + z[m3:]
        zr, zi = z[:, :g], z[:, g:]
        yh, yl = split(beside(zr * wc - zi * ws, zi * wc + zr * ws))
        reduced[b * m3 : (b + 1) * m3, :] = beside(yh, yl)
    xs = mm(reduced[...], dn_t[...])
    x = jnp.zeros(v.shape, f32)
    for b in range(thick):
        x = jnp.where(vlane == b, xs[b * m3 : (b + 1) * m3], x)
    ch, cl = split(x * below(pc, pc, pc))
    sh, sl = split(x * below(ps, ps, ps))
    coef = mm(beside(ch, cl, ch, sh, sl, sh), bo[...])
    qf, qa, t0, t1, t2 = (qs[k] for k in range(1, 6))
    va, vb, vc = [], [], []
    for al in range(3):
        rows = coef[al * nblk : (al + 1) * nblk]
        mid = []
        for be in range(3):
            h = []
            for ga in range(3):
                k = be * 3 + ga
                h.append(qa * rows[:, k : k + 1] + qf * rows[:, 9 + k : 10 + k])
            d2 = t2 * h[2]
            mid.append((h[0] + t2 * (h[1] + d2), h[1] + 2.0 * d2))
        d1 = t1 * mid[2][0]
        va.append(mid[0][0] + t1 * (mid[1][0] + d1))
        vb.append(mid[1][0] + 2.0 * d1)
        vc.append(mid[0][1] + t1 * (mid[1][1] + t1 * mid[2][1]))
    scale = 1.0 / (3.0 * exc)
    grad[0] = (va[1] + 2.0 * t0 * va[2]) * scale
    grad[1] = (vb[0] + t0 * (vb[1] + t0 * vb[2])) * scale
    grad[2] = (vc[0] + t0 * (vc[1] + t0 * vc[2])) * scale
    copy.wait()
    base = facts[0] * blocks
    sub8 = iota((8, 128), 0)
    mod4 = sub8 % 4
    for l in range(blocks):
        own = lambda q: qs[q, pl.ds(base + l, 1), :]
        fi, di, xi = own(1), own(2), [own(3 + c) for c in range(3)]
        me = own(0)
        size = xi[0] * xi[0] + xi[1] * xi[1] + xi[2] * xi[2] + soften_sq
        mine = jnp.where(sub8 == 3, 1.0, jnp.where(sub8 == 4, size, 0.0))
        for c in range(3):
            mine = jnp.where(sub8 == c, xi[c], mine)
        mh = mine.astype(bf16).astype(f32)
        left = jnp.transpose(below(mh, mh, mine - mh, jnp.zeros((104, 128), f32)))
        left = left[:, :32].astype(bf16)
        o = jnp.zeros((16, 128), f32)
        for first in range(0, slots, 2):
            right, sums = [], []
            for slot in range(first, min(first + 2, slots)):
                src = facts[1 + blocks + l * slots + slot]
                live = (slot < facts[1 + l]).astype(f32)
                away = qs[0, pl.ds(src, 1), :] - me
                fr, ad = qs[1, pl.ds(src, 1), :], qs[2, pl.ds(src, 1), :]
                xr = [qs[3 + c, pl.ds(src, 1), :] + away[:, 54 + c : 55 + c] for c in range(3)]
                sq = xr[0] * xr[0] + xr[1] * xr[1] + xr[2] * xr[2]
                moved = jnp.where(mod4 == 3, 1.0, jnp.where(mod4 == 2, xr[2], 0.0))
                moved = jnp.where(mod4 == 0, xr[0], jnp.where(mod4 == 1, xr[1], moved))
                other = jnp.where(sub8 == 3, sq, jnp.where(sub8 == 4, 1.0, 0.0))
                other = jnp.where(sub8 < 3, -2.0 * moved, other)
                oh = other.astype(bf16).astype(f32)
                right.append(below(oh, other - oh, oh, jnp.zeros((8, 128), f32)).astype(bf16))
                part = moved * jnp.where(sub8 < 4, fr * live, ad * live)
                ph = part.astype(bf16).astype(f32)
                sums.append(below(ph, part - ph).astype(bf16))
            inv = lax.rsqrt(mm(left, beside(*right)))
            ch, cl = split(inv * inv * inv)
            o = o + mm_nt(beside(*sums, *sums), beside(ch, cl))
        o = o[0:8] + o[8:16]
        for c in range(3):
            near = di * (o[c : c + 1] - xi[c] * o[3:4]) + fi * (o[4 + c : 5 + c] - xi[c] * o[7:8])
            grad[c, pl.ds(base + l, 1), :] += near * scale
    wrow = 4 * exc
    hrow = iota((wrow, 128), 0).astype(f32)
    lrow = iota((VCH, 128), 0).astype(f32)
    for k in range(3):
        vert = qs[6 + k].astype(jnp.int32)
        chunk, place = vert // VCH, vert % VCH
        qs[6 + k] = (chunk // slabs * 4 + chunk % 4).astype(f32)
        qs[k] = place.astype(f32)
    highs = []
    for c in range(3):
        h = grad[c].astype(bf16).astype(f32)
        qs[3 + c] = h
        grad[c] = grad[c] - h
    groups = slabs // 4
    acc = [[jnp.zeros((wrow, VCH), f32) for _ in range(groups)] for _ in range(3)]
    rmod = iota((wrow, VCH), 0) % 4
    for s in range(slabs):
        left, right = [], []
        for l in range(blocks):
            row = slice(s * blocks + l, s * blocks + l + 1)
            gs = [qs[3 + c, row, :] for c in range(3)] + [grad[c, row, :] for c in range(3)]
            for k in range(3):
                hit = hrow == qs[6 + k, row, :]
                left.append(below(*[jnp.where(hit, p, 0.0) for p in gs]).astype(bf16))
                right.append(jnp.where(lrow == qs[k, row, :], 1.0, 0.0).astype(bf16))
        tot = mm_nt(beside(*left), beside(*right))
        for c in range(3):
            part = tot[c * wrow : (c + 1) * wrow] + tot[(3 + c) * wrow : (4 + c) * wrow]
            q, r = s // 4, s % 4
            if r in (1, 2):
                acc[c][q] = acc[c][q] + part
            else:
                edge, to = (3, (q - 1) % groups) if r == 0 else (0, (q + 1) % groups)
                acc[c][to] = acc[c][to] + jnp.where(rmod == edge, part, 0.0)
                acc[c][q] = acc[c][q] + jnp.where(rmod == edge, 0.0, part)
    zero = jnp.zeros((wrow, 128 - 3 * VCH), f32)
    for q in range(groups):
        rows = beside(acc[0][q], acc[1][q], acc[2][q], zero)
        for e in range(exc):
            out[e * slabs + 4 * q : e * slabs + 4 * q + 4, :] = rows[4 * e : 4 * e + 4]


def sum_kernel(parts, out):
    row = jnp.sum(parts[...], axis=0, keepdims=True)
    for c in range(3):
        out[c : c + 1, :] = row[:, c * VCH : (c + 1) * VCH]


def on_device(
    q_forward, q_adjoint, panel_offset, block_anchor, kernel_hat, near_list, near_count,
    panel_vertices,
):
    slabs, exc = lax.axis_size("slab"), lax.axis_size("exc")
    blocks = block_anchor.shape[1]
    g, thick = kernel_hat.shape[0], kernel_hat.shape[1]
    nblk = slabs * blocks
    shape = lambda *s, t=f32: jax.ShapeDtypeStruct(s, t)
    params = pltpu.CompilerParams(vmem_limit_bytes=LIMIT)
    rows = QROWS * blocks
    packed = pl.pallas_call(
        functools.partial(pack_kernel, slabs, blocks),
        out_shape=shape(slabs, rows, 128),
        in_specs=[VM, VM, VM, SM, VM],
        out_specs=VM,
        scratch_shapes=[pltpu.VMEM((rows, 128), f32)],
        name="pack",
    )(q_forward, q_adjoint, panel_offset, block_anchor, panel_vertices)
    consts, prep_consts, lanes = tables(g, thick)
    lanes = jnp.asarray(lanes)
    slab = lax.axis_index("slab").astype(jnp.int32).reshape(1)
    facts = jnp.concatenate([slab, near_count, near_list.reshape(-1)])
    ready = pl.pallas_call(
        functools.partial(prep_kernel, thick),
        out_shape=(
            shape(thick, g, g), shape(thick, g // 2, g),
            shape(2, 384, 128, t=bf16), shape(768, 128, t=bf16), shape(g, 512, t=bf16),
        ),
        in_specs=[SM] + [VM] * 4,
        out_specs=(VM,) * 5,
        compiler_params=params,
        name="prep",
    )(facts, kernel_hat, *[jnp.asarray(c) for c in prep_consts], lanes)
    gathered = lax.all_to_all(packed, "slab", split_axis=0, concat_axis=0, tiled=True)
    partial = pl.pallas_call(
        functools.partial(main_kernel, slabs, exc, blocks, thick, g, near_list.shape[1]),
        out_shape=shape(exc * slabs, 128),
        in_specs=[pl.BlockSpec(memory_space=pl.ANY)] + [VM] * (7 + len(consts)),
        out_specs=VM,
        scratch_shapes=[
            pltpu.VMEM((QROWS, nblk, 128), f32),
            pltpu.VMEM((3, nblk, 128), f32),
            pltpu.VMEM((thick * 3 * nblk, 2 * g), f32),
            pltpu.VMEM((thick * 3 * nblk, 4 * g), bf16),
            pltpu.SMEM(facts.shape, jnp.int32),
            pltpu.SemaphoreType.DMA,
        ],
        compiler_params=params,
        name="field",
    )(facts, gathered, *ready, *[jnp.asarray(c) for c in consts], lanes)
    parts = lax.all_to_all(partial, ("exc", "slab"), split_axis=0, concat_axis=0, tiled=True)
    return pl.pallas_call(
        sum_kernel, out_shape=shape(3, VCH), in_specs=[VM], out_specs=VM,
        compiler_params=params, name="total",
    )(parts)


def solution(mesh):
    return jax.shard_map(
        on_device,
        mesh=mesh,
        in_specs=(
            P("exc", "slab"),
            P("exc", "slab"),
            P(None, "slab"),
            P(None, "slab"),
            P(None, "slab", None),
            P("slab", None),
            P("slab"),
            P(None, "slab"),
        ),
        out_specs=P(None, ("exc", "slab")),
        check_vma=False,
    )
```

```python
import functools
import math

import jax
import jax.numpy as jnp
import numpy as np
from jax import lax
from jax.experimental import pallas as pl
from jax.experimental.pallas import tpu as pltpu
from jax.sharding import PartitionSpec as P

VCH = 32
QROWS = 9
soften_sq = 16.0
bf16 = jnp.bfloat16
f32 = jnp.float32
VM = pl.BlockSpec(memory_space=pltpu.VMEM)
SM = pl.BlockSpec(memory_space=pltpu.SMEM)
LIMIT = 24 << 20


def split(x):
    high = x.astype(bf16)
    return high, (x - high.astype(f32)).astype(bf16)


def mm(a, b):
    return lax.dot_general(a, b, (((1,), (0,)), ((), ())), preferred_element_type=f32)


def mm_nt(a, b):
    return lax.dot_general(a, b, (((1,), (1,)), ((), ())), preferred_element_type=f32)


def beside(*parts):
    return jnp.concatenate(parts, axis=1)


def below(*parts):
    return jnp.concatenate(parts, axis=0)


def iota(shape, dim):
    return lax.broadcasted_iota(jnp.int32, shape, dim)


@functools.lru_cache(None)
def tables(g, thick):
    n = np.arange(g)
    ang = 2.0 * np.pi * (np.outer(n, n) % g) / g
    cos, sin = np.cos(ang), np.sin(ang)
    th = 2.0 * np.pi * n / g
    u = np.stack([np.ones(g), -1j * np.sin(th), np.cos(th) - 1.0])
    half = g // 2
    e = u[:, :, None] * (cos - 1j * sin)[None]
    rows = np.concatenate([e.real[:, : half + 1], -e.imag[:, 1:half]], axis=1)
    ct = np.concatenate([rows[k].T for k in range(3)], axis=1)
    cz = np.concatenate([cos, sin], axis=1)
    nb3 = 3 * thick
    up = np.zeros((64, 2 * g))
    dn = np.zeros((2 * g, 64))
    m = np.zeros((2, 3, 128, 64))
    bt = np.zeros((2, 3, 64, 128))
    for b in range(thick):
        for k in range(3):
            r, i = b * 3 + k, nb3 + b * 3 + k
            up[r, :g], up[r, g:] = u[k].real, u[k].imag
            up[i, :g], up[i, g:] = -u[k].imag, u[k].real
            uc = np.conj(u[k])
            dn[:g, r], dn[g:, r] = uc.real, -uc.imag
            dn[:g, i], dn[g:, i] = uc.imag, uc.real
            for al in range(3):
                f0, f1 = al * 9 + k, 27 + al * 9 + k
                m[0, 0, f0, r] = 1
                m[0, 0, f1, i] = 1
                m[0, 1, f0 + 3, i] = -1
                m[0, 1, f1 + 3, r] = 1
                m[0, 2, f0 + 6, r] = 1
                m[0, 2, f1 + 6, i] = 1
            bt[0, 0, r, k] = 1
            bt[0, 0, i, 9 + k] = 1
            bt[0, 1, r, 9 + 3 + k] = 1
            bt[0, 1, i, 3 + k] = -1
            bt[0, 2, r, 6 + k] = 1
            bt[0, 2, i, 9 + 6 + k] = 1
    real, imag = slice(0, nb3), slice(nb3, 2 * nb3)
    m[1, ..., real], m[1, ..., imag] = m[0, ..., imag], -m[0, ..., real]
    bt[1, :, real], bt[1, :, imag] = bt[0, :, imag], -bt[0, :, real]
    bt = bt / float(g) ** 3
    m = np.concatenate([m, m], axis=3)
    bt = np.concatenate([bt, bt], axis=2)
    lanes = np.full((64,), -1)
    lanes[: 2 * nb3] = np.tile(np.arange(thick).repeat(3), 2)
    lanes = np.tile(lanes, 2)[None]

    def halves(x):
        high = x.astype(np.float32).astype(bf16)
        return high, (x.astype(np.float32) - high.astype(np.float32)).astype(bf16)

    ct_h, ct_l = halves(ct)
    cz_h, cz_l = halves(cz)
    up_h, up_l = halves(up)
    dn_h, dn_l = halves(dn)
    up4 = np.concatenate([up_h, up_h, up_l, np.zeros_like(up_l)], axis=0)
    dn2 = np.concatenate([dn_h, dn_l], axis=1)
    ctz = np.concatenate([ct_h, ct_l], axis=1)
    czz = np.concatenate([cz_h, cz_l], axis=1)
    return (ctz, czz, up4, dn2), (m.astype(np.float32), bt.astype(np.float32)), lanes.astype(np.int32)


def pack_kernel(slabs, blocks, qf, qa, off, anchor, verts, out, buf):
    width = qf.shape[1] // blocks
    buf[...] = jnp.zeros_like(buf)
    for l in range(blocks):
        cut = slice(l * width, (l + 1) * width)
        buf[blocks + l : blocks + l + 1, :] = qf[:, cut]
        buf[2 * blocks + l : 2 * blocks + l + 1, :] = qa[:, cut]
        for c in range(3):
            row = (3 + c) * blocks + l
            buf[row : row + 1, :] = off[c : c + 1, cut]
            row = (6 + c) * blocks + l
            buf[row : row + 1, :] = verts[c : c + 1, cut].astype(f32)
    part = lambda q: buf[q * blocks : (q + 1) * blocks, :]
    t0, t1, t2 = part(3), part(4), part(5)
    lane = iota((blocks, 128), 1)
    sub = iota((blocks, 128), 0)
    acc = jnp.zeros((blocks, 128), f32)
    for f in range(2):
        x = part(1 + f)
        for al in range(3):
            y = x
            for be in range(3):
                z = y
                for ga in range(3):
                    idx = f * 27 + al * 9 + be * 3 + ga
                    acc = jnp.where(lane == idx, jnp.sum(z, axis=1, keepdims=True), acc)
                    z = z * t2
                y = y * t1
            x = x * t0
    for l in range(blocks):
        for c in range(3):
            hit = (lane == 54 + c) & (sub == l)
            acc = jnp.where(hit, anchor[c, l].astype(f32), acc)
    half = 4 * blocks
    halves = [below(acc, buf[blocks + h * half : blocks + (h + 1) * half, :]) for h in range(2)]
    for j in range(slabs):
        out[j] = halves[j % 2]


def prep_kernel(thick, k, m_t, bt_t, lane_t, ka, kd, mo, bo, fy):
    g = k.shape[0]
    half = g // 2
    for a in range(half):
        if a == 0:
            top, bot, dif = k[0], k[half], jnp.zeros_like(k[0])
        else:
            top = k[a] + k[g - a]
            bot, dif = top, k[a] - k[g - a]
        ka[:, a, :] = top
        ka[:, half + a, :] = bot
        kd[:, a, :] = dif
    freq = lane_t[...] + lax.axis_index("slab") * thick
    step = 2.0 * math.pi / g
    th = freq.astype(f32) * step
    sn, cm = jnp.sin(th), jnp.cos(th) - 1.0
    for v in range(2):
        h, l = split(m_t[v, 0] + m_t[v, 1] * sn + m_t[v, 2] * cm)
        mo[v] = below(h, h, l)
    pieces = []
    for v in range(2):
        h, l = split(bt_t[v, 0] + bt_t[v, 1] * jnp.transpose(jnp.broadcast_to(sn, (128, 128)))
                     + bt_t[v, 2] * jnp.transpose(jnp.broadcast_to(cm, (128, 128))))
        pieces += [h, h, l]
    bo[...] = below(*pieces)
    turn = ((iota((g, 128), 0) * freq) & (g - 1)).astype(f32) * step
    ch, cl = split(jnp.cos(turn))
    sh, sl = split(jnp.sin(turn))
    fy[...] = beside(ch, sh, cl, sl)


def stagger(count, *stages):
    for step in range(count + len(stages) - 1):
        for k, stage in enumerate(stages):
            if 0 <= step - k < count:
                stage(step - k)
        yield


def spectrum_kernel(
    slabs, blocks, thick, g,
    gat, ka, kd, mo, bo, fy, ct_t, cz_t, up_t, dn_t, lane_t,
    out, head_ref, expand,
):
    nblk = slabs * blocks
    half = g // 2
    for s in range(slabs):
        head_ref[s * blocks : (s + 1) * blocks, :] = gat[s, 0:blocks, :]
    head = head_ref[...]
    lane = iota((nblk, 128), 1)
    glane = iota((nblk, g), 1).astype(f32)
    hot = lambda c: jnp.where(glane == head[:, 54 + c : 55 + c], 1.0, 0.0).astype(bf16)
    ph = mm(hot(1), fy[...])
    ph = ph[:, :256] + ph[:, 256:]
    pc, ps = ph[:, :128], ph[:, 128:]
    vs = []
    for al in range(3):
        lo, hi = al * 9, al * 9 + 9
        keep = ((lane >= lo) & (lane < hi)) | ((lane >= 27 + lo) & (lane < 27 + hi))
        h, l = split(jnp.where(keep, head, 0.0))
        q3 = beside(h, l, h)
        vs.append(mm(q3, mo[0]) * pc + mm(q3, mo[1]) * ps)
    v = below(*vs)
    vh = v.astype(bf16).astype(f32)
    v = jnp.where(iota(v.shape, 1) < 64, vh, v - vh)
    vlane = lane_t[...]
    m3 = 3 * nblk
    vb = below(*[jnp.where(vlane == b, v, 0.0) for b in range(thick)]).astype(bf16)
    expand[...] = mm(beside(vb, vb), up_t[...])
    cth = mm(hot(0), ct_t[...])
    rows3 = lambda x, o: below(*[x[:, o + k * g : o + (k + 1) * g] for k in range(3)])
    ct_h, ct_l = rows3(cth, 0), rows3(cth, 3 * g)
    cc_h = jnp.transpose(ct_h).astype(bf16)
    cc = below(cc_h, jnp.transpose(ct_l).astype(bf16))
    ct_h, ct_l = ct_h.astype(bf16), ct_l.astype(bf16)
    ct = below(beside(ct_h, ct_h), beside(ct_l, jnp.zeros_like(ct_l)))
    wz = mm(hot(2), cz_t[...])
    wz = wz[:, : 2 * g] + wz[:, 2 * g :]
    wc = below(*[wz[:, :g]] * 3)
    ws = below(*[wz[:, g:]] * 3)
    hold = {"x": jnp.zeros(v.shape, f32)}

    def forward(b):
        ar, ai = expand[b * m3 : (b + 1) * m3, :g], expand[b * m3 : (b + 1) * m3, g:]
        rh, rl = split(beside(ar * wc + ai * ws, ai * wc - ar * ws))
        pn = mm(cc, rh)
        hold["pn", b] = pn[:g] + pn[g:] + mm(cc_h, rl)

    def backward(b):
        pn = hold.pop(("pn", b))
        pr, pi = pn[:half, :g], pn[:half, g:]
        nr, ni = pn[half:, :g], pn[half:, g:]
        kt, kb, kx = ka[b, :half, :], ka[b, half:, :], kd[b]
        top = beside(pr * kt + ni * kx, pi * kt - nr * kx)
        bot = beside(nr * kb - pi * kx, ni * kb + pr * kx)
        th, tl = split(below(top, bot))
        z = mm(ct, below(th, tl))
        hold["z", b] = z[:m3] + z[m3:]

    def reduce(b):
        z = hold.pop(("z", b))
        zr, zi = z[:, :g], z[:, g:]
        yh, yl = split(beside(zr * wc - zi * ws, zi * wc + zr * ws))
        xs = mm(below(yh, yl), dn_t[...])
        hold["x"] = jnp.where(vlane == b, xs[:m3] + xs[m3:], hold["x"])

    for _ in stagger(thick, forward, backward, reduce):
        pass
    x = hold["x"]
    ch, cl = split(x * below(pc, pc, pc))
    sh, sl = split(x * below(ps, ps, ps))
    out[...] = mm(beside(ch, cl, ch, sh, sl, sh), bo[...])


def panel_kernel(
    slabs, exc, blocks, slots,
    facts_any, gat, swapped, coef,
    out, qs, grad, facts, sem,
):
    copy = pltpu.make_async_copy(facts_any, facts, sem)
    copy.start()
    nblk = slabs * blocks
    slab = lax.axis_index("slab")
    for s in range(slabs):
        qs[0, s * blocks : (s + 1) * blocks, :] = gat[s, 0:blocks, :]

    def regroup(first, second):
        for s in range(slabs):
            for q in range(4):
                rows, to = slice((q + 1) * blocks, (q + 2) * blocks), slice(s * blocks, (s + 1) * blocks)
                qs[1 + q, to, :] = first[s, rows, :]
                qs[5 + q, to, :] = second[s, rows, :]

    pl.when(slab % 2 == 0)(lambda: regroup(gat, swapped))
    pl.when(slab % 2 == 1)(lambda: regroup(swapped, gat))
    copy.wait()
    base = slab * blocks
    sub8 = iota((8, 128), 0)
    mod4 = sub8 % 4
    scale = 1.0 / (3.0 * exc)
    pairs = -(-slots // 2)
    hold, mine_of = {}, {}

    def gather_pair(n):
        l, first = n // pairs, n % pairs * 2
        if first == 0:
            own = lambda q: qs[q, pl.ds(base + l, 1), :]
            fi, di, xi, me = own(1), own(2), [own(3 + c) for c in range(3)], own(0)
            size = xi[0] * xi[0] + xi[1] * xi[1] + xi[2] * xi[2] + soften_sq
            mine = jnp.where(sub8 == 3, 1.0, jnp.where(sub8 == 4, size, 0.0))
            for c in range(3):
                mine = jnp.where(sub8 == c, xi[c], mine)
            mh = mine.astype(bf16).astype(f32)
            left = jnp.transpose(below(mh, mh, mine - mh, jnp.zeros((104, 128), f32)))
            mine_of[l] = (fi, di, xi, me, left[:, :32].astype(bf16))
            hold["o", l] = jnp.zeros((16, 128), f32)
        me = mine_of[l][3]
        right, sums = [], []
        for slot in range(first, min(first + 2, slots)):
            src = facts[blocks + l * slots + slot]
            live = (slot < facts[l]).astype(f32)
            away = qs[0, pl.ds(src, 1), :] - me
            fr, ad = qs[1, pl.ds(src, 1), :], qs[2, pl.ds(src, 1), :]
            xr = [qs[3 + c, pl.ds(src, 1), :] + away[:, 54 + c : 55 + c] for c in range(3)]
            sq = xr[0] * xr[0] + xr[1] * xr[1] + xr[2] * xr[2]
            moved = jnp.where(mod4 == 3, 1.0, jnp.where(mod4 == 2, xr[2], 0.0))
            moved = jnp.where(mod4 == 0, xr[0], jnp.where(mod4 == 1, xr[1], moved))
            other = jnp.where(sub8 == 3, sq, jnp.where(sub8 == 4, 1.0, 0.0))
            other = jnp.where(sub8 < 3, -2.0 * moved, other)
            oh = other.astype(bf16).astype(f32)
            right.append(below(oh, other - oh, oh, jnp.zeros((8, 128), f32)).astype(bf16))
            part = moved * jnp.where(sub8 < 4, fr * live, ad * live)
            ph = part.astype(bf16).astype(f32)
            sums.append(below(ph, part - ph).astype(bf16))
        hold["right", n] = beside(*right)
        hold["sums", n] = beside(*sums, *sums)

    def distance_pair(n):
        hold["d", n] = mm(mine_of[n // pairs][4], hold.pop(("right", n)))

    def cube_pair(n):
        inv = lax.rsqrt(hold.pop(("d", n)))
        hold["cube", n] = beside(*split(inv * inv * inv))

    def sum_pair(n):
        l = n // pairs
        hold["o", l] = hold["o", l] + mm_nt(hold.pop(("sums", n)), hold.pop(("cube", n)))

    near_steps = stagger(blocks * pairs, gather_pair, distance_pair, cube_pair, sum_pair)
    qf, qa, t0, t1, t2 = (qs[k] for k in range(1, 6))
    va, vb, vc = [], [], []
    for al in range(3):
        rows = coef[al * nblk : (al + 1) * nblk, :]
        mid = []
        for be in range(3):
            h = []
            for ga in range(3):
                k = be * 3 + ga
                h.append(qa * rows[:, k : k + 1] + qf * rows[:, 9 + k : 10 + k])
            d2 = t2 * h[2]
            mid.append((h[0] + t2 * (h[1] + d2), h[1] + 2.0 * d2))
            next(near_steps, None)
            next(near_steps, None)
        d1 = t1 * mid[2][0]
        va.append(mid[0][0] + t1 * (mid[1][0] + d1))
        vb.append(mid[1][0] + 2.0 * d1)
        vc.append(mid[0][1] + t1 * (mid[1][1] + t1 * mid[2][1]))
    for _ in near_steps:
        pass
    grad[0] = (va[1] + 2.0 * t0 * va[2]) * scale
    grad[1] = (vb[0] + t0 * (vb[1] + t0 * vb[2])) * scale
    grad[2] = (vc[0] + t0 * (vc[1] + t0 * vc[2])) * scale
    for l in range(blocks):
        fi, di, xi = mine_of[l][:3]
        o = hold["o", l]
        o = o[0:8] + o[8:16]
        for c in range(3):
            near = di * (o[c : c + 1] - xi[c] * o[3:4]) + fi * (o[4 + c : 5 + c] - xi[c] * o[7:8])
            grad[c, pl.ds(base + l, 1), :] += near * scale
    wrow = 4 * exc
    hrow = iota((wrow, 128), 0).astype(f32)
    lrow = iota((VCH, 128), 0).astype(f32)
    for k in range(3):
        vert = qs[6 + k].astype(jnp.int32)
        chunk, place = vert // VCH, vert % VCH
        qs[6 + k] = (chunk // slabs * 4 + chunk % 4).astype(f32)
        qs[k] = place.astype(f32)
    highs = []
    for c in range(3):
        h = grad[c].astype(bf16).astype(f32)
        qs[3 + c] = h
        grad[c] = grad[c] - h
    groups = slabs // 4
    acc = [[jnp.zeros((wrow, VCH), f32) for _ in range(groups)] for _ in range(3)]
    rmod = iota((wrow, VCH), 0) % 4
    for s in range(slabs):
        left, right = [], []
        for l in range(blocks):
            row = slice(s * blocks + l, s * blocks + l + 1)
            gs = [qs[3 + c, row, :] for c in range(3)] + [grad[c, row, :] for c in range(3)]
            for k in range(3):
                hit = hrow == qs[6 + k, row, :]
                left.append(below(*[jnp.where(hit, p, 0.0) for p in gs]).astype(bf16))
                right.append(jnp.where(lrow == qs[k, row, :], 1.0, 0.0).astype(bf16))
        tot = mm_nt(beside(*left), beside(*right))
        for c in range(3):
            part = tot[c * wrow : (c + 1) * wrow] + tot[(3 + c) * wrow : (4 + c) * wrow]
            q, r = s // 4, s % 4
            if r in (1, 2):
                acc[c][q] = acc[c][q] + part
            else:
                edge, to = (3, (q - 1) % groups) if r == 0 else (0, (q + 1) % groups)
                acc[c][to] = acc[c][to] + jnp.where(rmod == edge, part, 0.0)
                acc[c][q] = acc[c][q] + jnp.where(rmod == edge, 0.0, part)
    zero = jnp.zeros((wrow, 128 - 3 * VCH), f32)
    for q in range(groups):
        rows = beside(acc[0][q], acc[1][q], acc[2][q], zero)
        for e in range(exc):
            out[e * slabs + 4 * q : e * slabs + 4 * q + 4, :] = rows[4 * e : 4 * e + 4]


def sum_kernel(parts, out):
    row = jnp.sum(parts[...], axis=0, keepdims=True)
    for c in range(3):
        out[c : c + 1, :] = row[:, c * VCH : (c + 1) * VCH]


def on_device(
    q_forward, q_adjoint, panel_offset, block_anchor, kernel_hat, near_list, near_count,
    panel_vertices,
):
    slabs, exc = lax.axis_size("slab"), lax.axis_size("exc")
    blocks = block_anchor.shape[1]
    g, thick = kernel_hat.shape[0], kernel_hat.shape[1]
    nblk = slabs * blocks
    shape = lambda *s, t=f32: jax.ShapeDtypeStruct(s, t)
    params = pltpu.CompilerParams(vmem_limit_bytes=LIMIT)
    rows = QROWS * blocks
    packed = pl.pallas_call(
        functools.partial(pack_kernel, slabs, blocks),
        out_shape=shape(slabs, 5 * blocks, 128),
        in_specs=[VM, VM, VM, SM, VM],
        out_specs=VM,
        scratch_shapes=[pltpu.VMEM((rows, 128), f32)],
        name="pack",
    )(q_forward, q_adjoint, panel_offset, block_anchor, panel_vertices)
    consts, prep_consts, lanes = tables(g, thick)
    lanes = jnp.asarray(lanes)
    facts = jnp.concatenate([near_count, near_list.reshape(-1)])
    ready = pl.pallas_call(
        functools.partial(prep_kernel, thick),
        out_shape=(
            shape(thick, g, g), shape(thick, g // 2, g),
            shape(2, 384, 128, t=bf16), shape(768, 128, t=bf16), shape(g, 512, t=bf16),
        ),
        in_specs=[VM] * 4,
        out_specs=(VM,) * 5,
        compiler_params=params,
        name="prep",
    )(kernel_hat, *[jnp.asarray(c) for c in prep_consts], lanes)
    gathered = lax.all_to_all(packed, "slab", split_axis=0, concat_axis=0, tiled=True)
    swapped = lax.ppermute(gathered, "slab", [(i, i ^ 1) for i in range(slabs)])
    coef = pl.pallas_call(
        functools.partial(spectrum_kernel, slabs, blocks, thick, g),
        out_shape=shape(3 * nblk, 128),
        in_specs=[VM] * (7 + len(consts)),
        out_specs=VM,
        scratch_shapes=[
            pltpu.VMEM((nblk, 128), f32),
            pltpu.VMEM((thick * 3 * nblk, 2 * g), f32),
        ],
        compiler_params=params,
        cost_estimate=pl.CostEstimate(flops=10**9, bytes_accessed=2 * 10**6, transcendentals=0),
        name="spectrum",
    )(gathered, *ready, *[jnp.asarray(c) for c in consts], lanes)
    partial = pl.pallas_call(
        functools.partial(panel_kernel, slabs, exc, blocks, near_list.shape[1]),
        out_shape=shape(exc * slabs, 128),
        in_specs=[pl.BlockSpec(memory_space=pl.ANY)] + [VM] * 3,
        out_specs=VM,
        scratch_shapes=[
            pltpu.VMEM((QROWS, nblk, 128), f32),
            pltpu.VMEM((3, nblk, 128), f32),
            pltpu.SMEM(facts.shape, jnp.int32),
            pltpu.SemaphoreType.DMA,
        ],
        compiler_params=params,
        name="panel",
    )(facts, gathered, swapped, coef)
    parts = lax.all_to_all(partial, ("exc", "slab"), split_axis=0, concat_axis=0, tiled=True)
    return pl.pallas_call(
        sum_kernel, out_shape=shape(3, VCH), in_specs=[VM], out_specs=VM,
        compiler_params=params, name="total",
    )(parts)


def solution(mesh):
    return jax.shard_map(
        on_device,
        mesh=mesh,
        in_specs=(
            P("exc", "slab"),
            P("exc", "slab"),
            P(None, "slab"),
            P(None, "slab"),
            P(None, "slab", None),
            P("slab", None),
            P("slab"),
            P(None, "slab"),
        ),
        out_specs=P(None, ("exc", "slab")),
        check_vma=False,
    )
```

```python
import functools
import math

import jax
import jax.numpy as jnp
import numpy as np
from jax import lax
from jax.experimental import pallas as pl
from jax.experimental.pallas import tpu as pltpu
from jax.sharding import PartitionSpec as P

VCH = 32
QROWS = 9
soften_sq = 16.0
bf16 = jnp.bfloat16
f32 = jnp.float32
VM = pl.BlockSpec(memory_space=pltpu.VMEM)
SM = pl.BlockSpec(memory_space=pltpu.SMEM)
LIMIT = 24 << 20


def split(x):
    high = x.astype(bf16)
    return high, (x - high.astype(f32)).astype(bf16)


def mm(a, b):
    return lax.dot_general(a, b, (((1,), (0,)), ((), ())), preferred_element_type=f32)


def mm_nt(a, b):
    return lax.dot_general(a, b, (((1,), (1,)), ((), ())), preferred_element_type=f32)


def beside(*parts):
    return jnp.concatenate(parts, axis=1)


def below(*parts):
    return jnp.concatenate(parts, axis=0)


def iota(shape, dim):
    return lax.broadcasted_iota(jnp.int32, shape, dim)


@functools.lru_cache(None)
def tables(g, thick):
    n = np.arange(g)
    ang = 2.0 * np.pi * (np.outer(n, n) % g) / g
    cos, sin = np.cos(ang), np.sin(ang)
    th = 2.0 * np.pi * n / g
    u = np.stack([np.ones(g), -1j * np.sin(th), np.cos(th) - 1.0])
    half = g // 2
    e = u[:, :, None] * (cos - 1j * sin)[None]
    rows = np.concatenate([e.real[:, : half + 1], -e.imag[:, 1:half]], axis=1)
    ct = np.concatenate([rows[k].T for k in range(3)], axis=1)
    cz = np.concatenate([cos, sin], axis=1)
    nb3 = 3 * thick
    up = np.zeros((64, 2 * g))
    dn = np.zeros((2 * g, 64))
    m = np.zeros((2, 3, 128, 64))
    bt = np.zeros((2, 3, 64, 128))
    for b in range(thick):
        for k in range(3):
            r, i = b * 3 + k, nb3 + b * 3 + k
            up[r, :g], up[r, g:] = u[k].real, u[k].imag
            up[i, :g], up[i, g:] = -u[k].imag, u[k].real
            uc = np.conj(u[k])
            dn[:g, r], dn[g:, r] = uc.real, -uc.imag
            dn[:g, i], dn[g:, i] = uc.imag, uc.real
            for al in range(3):
                f0, f1 = al * 9 + k, 27 + al * 9 + k
                m[0, 0, f0, r] = 1
                m[0, 0, f1, i] = 1
                m[0, 1, f0 + 3, i] = -1
                m[0, 1, f1 + 3, r] = 1
                m[0, 2, f0 + 6, r] = 1
                m[0, 2, f1 + 6, i] = 1
            bt[0, 0, r, k] = 1
            bt[0, 0, i, 9 + k] = 1
            bt[0, 1, r, 9 + 3 + k] = 1
            bt[0, 1, i, 3 + k] = -1
            bt[0, 2, r, 6 + k] = 1
            bt[0, 2, i, 9 + 6 + k] = 1
    bt[..., 64:] = bt[..., :64]
    real, imag = slice(0, nb3), slice(nb3, 2 * nb3)
    m[1, ..., real], m[1, ..., imag] = m[0, ..., imag], -m[0, ..., real]
    bt[1, :, real], bt[1, :, imag] = bt[0, :, imag], -bt[0, :, real]
    bt = bt / float(g) ** 3
    m = np.concatenate([m, m], axis=3)
    bt = np.concatenate([bt, bt], axis=2)
    lanes = np.full((64,), -1)
    lanes[: 2 * nb3] = np.tile(np.arange(thick).repeat(3), 2)
    lanes = np.tile(lanes, 2)[None]

    def halves(x):
        high = x.astype(np.float32).astype(bf16)
        return high, (x.astype(np.float32) - high.astype(np.float32)).astype(bf16)

    ct_h, ct_l = halves(ct)
    cz_h, cz_l = halves(cz)
    up_h, up_l = halves(up)
    dn_h, dn_l = halves(dn)
    up4 = np.concatenate([up_h, up_h, up_l, np.zeros_like(up_l)], axis=0)
    dn2 = np.concatenate([dn_h, dn_l], axis=1)
    ctz = np.concatenate([ct_h, ct_l], axis=1)
    czz = np.concatenate([cz_h, cz_l], axis=1)
    return (ctz, czz, up4, dn2), (m.astype(np.float32), bt.astype(np.float32)), lanes.astype(np.int32)


def pack_kernel(slabs, blocks, qf, qa, off, anchor, verts, out, buf):
    width = qf.shape[1] // blocks
    buf[...] = jnp.zeros_like(buf)
    for l in range(blocks):
        cut = slice(l * width, (l + 1) * width)
        buf[blocks + l : blocks + l + 1, :] = qf[:, cut]
        buf[2 * blocks + l : 2 * blocks + l + 1, :] = qa[:, cut]
        for c in range(3):
            row = (3 + c) * blocks + l
            buf[row : row + 1, :] = off[c : c + 1, cut]
            row = (6 + c) * blocks + l
            buf[row : row + 1, :] = verts[c : c + 1, cut].astype(f32)
    part = lambda q: buf[q * blocks : (q + 1) * blocks, :]
    t0, t1, t2 = part(3), part(4), part(5)
    lane = iota((blocks, 128), 1)
    sub = iota((blocks, 128), 0)
    acc = jnp.zeros((blocks, 128), f32)
    for f in range(2):
        x = part(1 + f)
        for al in range(3):
            y = x
            for be in range(3):
                z = y
                for ga in range(3):
                    idx = f * 27 + al * 9 + be * 3 + ga
                    acc = jnp.where(lane == idx, jnp.sum(z, axis=1, keepdims=True), acc)
                    z = z * t2
                y = y * t1
            x = x * t0
    for l in range(blocks):
        for c in range(3):
            hit = (lane == 54 + c) & (sub == l)
            acc = jnp.where(hit, anchor[c, l].astype(f32), acc)
    pieces = [acc] + [part(q) for q in range(1, QROWS)]
    for j in range(slabs):
        out[j, 0] = acc
        for q in range(4):
            out[j, 1 + q] = pieces[1 + j % 2 * 4 + q]


def prep_kernel(thick, k, m_t, bt_t, lane_t, ka, kd, mo, bo, fy):
    g = k.shape[0]
    half = g // 2
    for a in range(half):
        if a == 0:
            top, bot, dif = k[0], k[half], jnp.zeros_like(k[0])
        else:
            top = k[a] + k[g - a]
            bot, dif = top, k[a] - k[g - a]
        ka[:, a, :] = top
        ka[:, half + a, :] = bot
        kd[:, a, :] = dif
    freq = lane_t[...] + lax.axis_index("slab") * thick
    step = 2.0 * math.pi / g
    th = freq.astype(f32) * step
    sn, cm = jnp.sin(th), jnp.cos(th) - 1.0
    forms = [m_t[v, 0] + m_t[v, 1] * sn + m_t[v, 2] * cm for v in range(2)]
    h, l = split(beside(*forms))
    mo[...] = below(h, h, l)
    down = lambda row: jnp.transpose(jnp.broadcast_to(row, (128, 128)))
    sn, cm = down(sn), down(cm)
    h, l = split(below(*[bt_t[v, 0] + bt_t[v, 1] * sn + bt_t[v, 2] * cm for v in range(2)]))
    bo[...] = jnp.where(iota(h.shape, 1) < 64, h.astype(f32), l.astype(f32)).astype(bf16)
    turn = ((iota((g, 128), 0) * freq) & (g - 1)).astype(f32) * step
    ch, cl = split(jnp.cos(turn))
    sh, sl = split(jnp.sin(turn))
    fy[...] = beside(ch, sh, cl, sl)


def stagger(count, *stages):
    for step in range(count + len(stages) - 1):
        for k, stage in enumerate(stages):
            if 0 <= step - k < count:
                stage(step - k)
        yield


def spectrum_kernel(
    slabs, blocks, thick, g,
    gat, ka, kd, mo, bo, fy, ct_t, cz_t, up_t, dn_t, lane_t,
    out, head_ref, expand,
):
    nblk = slabs * blocks
    half = g // 2
    for s in range(slabs):
        head_ref[s * blocks : (s + 1) * blocks, :] = gat[s, 0]
    head = head_ref[...]
    lane = iota((nblk, 128), 1)
    glane = iota((nblk, g), 1).astype(f32)
    hot = lambda c: jnp.where(glane == head[:, 54 + c : 55 + c], 1.0, 0.0).astype(bf16)
    ph = mm(hot(1), fy[...])
    ph = ph[:, :256] + ph[:, 256:]
    pc, ps = ph[:, :128], ph[:, 128:]
    qs = []
    for al in range(3):
        lo, hi = al * 9, al * 9 + 9
        keep = ((lane >= lo) & (lane < hi)) | ((lane >= 27 + lo) & (lane < 27 + hi))
        h, l = split(jnp.where(keep, head, 0.0))
        qs.append(beside(h, l, h))
    v = mm(below(*qs), mo[...])
    v = v[:, :128] * below(pc, pc, pc) + v[:, 128:] * below(ps, ps, ps)
    vh = v.astype(bf16).astype(f32)
    v = jnp.where(iota(v.shape, 1) < 64, vh, v - vh)
    vlane = lane_t[...]
    m3 = 3 * nblk
    vb = below(*[jnp.where(vlane == b, v, 0.0) for b in range(thick)]).astype(bf16)
    expand[...] = mm(beside(vb, vb), up_t[...])
    cth = mm(hot(0), ct_t[...])
    rows3 = lambda x, o: below(*[x[:, o + k * g : o + (k + 1) * g] for k in range(3)])
    ct_h, ct_l = rows3(cth, 0), rows3(cth, 3 * g)
    cc_h = jnp.transpose(ct_h).astype(bf16)
    cc = below(cc_h, jnp.transpose(ct_l).astype(bf16))
    ct_h, ct_l = ct_h.astype(bf16), ct_l.astype(bf16)
    ct = below(beside(ct_h, ct_h), beside(ct_l, jnp.zeros_like(ct_l)))
    wz = mm(hot(2), cz_t[...])
    wz = wz[:, : 2 * g] + wz[:, 2 * g :]
    wc = below(*[wz[:, :g]] * 3)
    ws = below(*[wz[:, g:]] * 3)
    hold = {"x": jnp.zeros(v.shape, f32)}

    def forward(b):
        ar, ai = expand[b * m3 : (b + 1) * m3, :g], expand[b * m3 : (b + 1) * m3, g:]
        rh, rl = split(beside(ar * wc + ai * ws, ai * wc - ar * ws))
        pn = mm(cc, rh)
        hold["pn", b] = pn[:g] + pn[g:] + mm(cc_h, rl)

    def backward(b):
        pn = hold.pop(("pn", b))
        pr, pi = pn[:half, :g], pn[:half, g:]
        nr, ni = pn[half:, :g], pn[half:, g:]
        kt, kb, kx = ka[b, :half, :], ka[b, half:, :], kd[b]
        top = beside(pr * kt + ni * kx, pi * kt - nr * kx)
        bot = beside(nr * kb - pi * kx, ni * kb + pr * kx)
        th, tl = split(below(top, bot))
        z = mm(ct, below(th, tl))
        hold["z", b] = z[:m3] + z[m3:]

    def reduce(b):
        z = hold.pop(("z", b))
        zr, zi = z[:, :g], z[:, g:]
        hold["y", b] = split(beside(zr * wc - zi * ws, zi * wc + zr * ws))
        if b % 2 or b == thick - 1:
            both = [hold.pop(("y", k)) for k in range(b - b % 2, b + 1)]
            xs = mm(below(*[half for y in both for half in y]), dn_t[...])
            for k in range(len(both)):
                sums = xs[2 * k * m3 : (2 * k + 1) * m3] + xs[(2 * k + 1) * m3 : (2 * k + 2) * m3]
                hold["x"] = jnp.where(vlane == b - b % 2 + k, sums, hold["x"])

    for _ in stagger(thick, forward, backward, reduce):
        pass
    x = hold["x"]
    h, l = split(beside(x * below(pc, pc, pc), x * below(ps, ps, ps)))
    coef = mm(below(h, l), bo[...])
    coef = coef[:m3] + coef[m3:]
    out[...] = coef + pltpu.roll(coef, 64, 1)


def panel_kernel(
    slabs, exc, blocks, slots,
    facts_any, gat, swapped, coef,
    out, qs, verts, grad, facts, sem,
):
    copy = pltpu.make_async_copy(facts_any, facts, sem)
    copy.start()
    nblk = slabs * blocks
    slab = lax.axis_index("slab")
    for s in range(slabs):
        qs[0, s * blocks : (s + 1) * blocks, :] = gat[s, 0]

    def regroup(first, second):
        for s in range(slabs):
            for q in range(4):
                to = slice(s * blocks, (s + 1) * blocks)
                qs[1 + q, to, :] = first[s, 1 + q]
                qs[5 + q, to, :] = second[s, 1 + q]

    pl.when(slab % 2 == 0)(lambda: regroup(gat, swapped))
    pl.when(slab % 2 == 1)(lambda: regroup(swapped, gat))
    copy.wait()
    base = slab * blocks
    sub8 = iota((8, 128), 0)
    mod4 = sub8 % 4
    scale = 1.0 / (3.0 * exc)
    pairs = -(-slots // 2)
    hold, mine_of = {}, {}

    def gather_pair(n):
        l, first = n // pairs, n % pairs * 2
        if first == 0:
            own = lambda q: qs[q, pl.ds(base + l, 1), :]
            fi, di, xi, me = own(1), own(2), [own(3 + c) for c in range(3)], own(0)
            size = xi[0] * xi[0] + xi[1] * xi[1] + xi[2] * xi[2] + soften_sq
            mine = jnp.where(sub8 == 3, 1.0, jnp.where(sub8 == 4, size, 0.0))
            for c in range(3):
                mine = jnp.where(sub8 == c, xi[c], mine)
            mh = mine.astype(bf16).astype(f32)
            left = jnp.transpose(below(mh, mh, mine - mh, jnp.zeros((104, 128), f32)))
            mine_of[l] = (fi, di, xi, me, left[:, :32].astype(bf16))
            hold["o", l] = jnp.zeros((16, 128), f32)
        me = mine_of[l][3]
        right, sums = [], []
        for slot in range(first, min(first + 2, slots)):
            src = facts[blocks + l * slots + slot]
            live = (slot < facts[l]).astype(f32)
            away = qs[0, pl.ds(src, 1), :] - me
            fr, ad = qs[1, pl.ds(src, 1), :], qs[2, pl.ds(src, 1), :]
            xr = [qs[3 + c, pl.ds(src, 1), :] + away[:, 54 + c : 55 + c] for c in range(3)]
            sq = xr[0] * xr[0] + xr[1] * xr[1] + xr[2] * xr[2]
            moved = jnp.where(mod4 == 3, 1.0, jnp.where(mod4 == 2, xr[2], 0.0))
            moved = jnp.where(mod4 == 0, xr[0], jnp.where(mod4 == 1, xr[1], moved))
            other = jnp.where(sub8 == 3, sq, jnp.where(sub8 == 4, 1.0, 0.0))
            other = jnp.where(sub8 < 3, -2.0 * moved, other)
            oh = other.astype(bf16).astype(f32)
            right.append(below(oh, other - oh, oh, jnp.zeros((8, 128), f32)).astype(bf16))
            part = moved * jnp.where(sub8 < 4, fr * live, ad * live)
            ph = part.astype(bf16).astype(f32)
            sums.append(below(ph, part - ph).astype(bf16))
        hold["right", n] = beside(*right)
        hold["sums", n] = beside(*sums, *sums)

    def distance_pair(n):
        hold["d", n] = mm(mine_of[n // pairs][4], hold.pop(("right", n)))

    def cube_pair(n):
        inv = lax.rsqrt(hold.pop(("d", n)))
        hold["cube", n] = beside(*split(inv * inv * inv))

    def sum_pair(n):
        l = n // pairs
        hold["o", l] = hold["o", l] + mm_nt(hold.pop(("sums", n)), hold.pop(("cube", n)))

    near_steps = stagger(blocks * pairs, gather_pair, distance_pair, cube_pair, sum_pair)
    wrow = 4 * exc
    hrow = iota((wrow, 128), 0).astype(f32)
    lrow = iota((VCH, 128), 0).astype(f32)
    rmod = iota((wrow, VCH), 0) % 4
    groups = slabs // 4
    acc = [[jnp.zeros((wrow, VCH), f32) for _ in range(groups)] for _ in range(3)]

    def far_steps(group):
        to = slice(group * 4 * blocks, (group + 1) * 4 * blocks)
        qf, qa, t0, t1, t2 = (qs[k, to, :] for k in range(1, 6))
        va, vb, vc = [], [], []
        for al in range(3):
            rows = coef[al * nblk + to.start : al * nblk + to.stop, :]
            mid = []
            for be in range(3):
                h = []
                for ga in range(3):
                    k = be * 3 + ga
                    h.append(qa * rows[:, k : k + 1] + qf * rows[:, 9 + k : 10 + k])
                d2 = t2 * h[2]
                e2 = h[1] + d2
                mid.append((h[0] + t2 * e2, e2 + d2))
                yield
            d1 = t1 * mid[2][0]
            e1 = mid[1][0] + d1
            va.append(mid[0][0] + t1 * e1)
            vb.append(e1 + d1)
            vc.append(mid[0][1] + t1 * (mid[1][1] + t1 * mid[2][1]))
        total = (
            va[1] + 2.0 * t0 * va[2],
            vb[0] + t0 * (vb[1] + t0 * vb[2]),
            vc[0] + t0 * (vc[1] + t0 * vc[2]),
        )
        for c in range(3):
            value = total[c] * scale
            high = value.astype(bf16).astype(f32)
            grad[c, to, :] = high
            grad[3 + c, to, :] = value - high
        for k in range(3):
            vert = qs[6 + k, to, :]
            chunk = jnp.floor((vert + 0.5) * (1.0 / VCH))
            part = jnp.floor((chunk + 0.5) * (1.0 / slabs))
            verts[k, to, :] = 4.0 * part + (chunk - 4.0 * jnp.floor(chunk * 0.25))
            verts[3 + k, to, :] = vert - float(VCH) * chunk

    def vertex_sums(values_of, row_of):
        left, right = [], []
        for l in range(blocks):
            values, row = values_of(l), row_of(l)
            for k in range(3):
                hit = hrow == verts[k, row, :]
                left.append(below(*[jnp.where(hit, p, 0.0) for p in values]).astype(bf16))
                right.append(jnp.where(lrow == verts[3 + k, row, :], 1.0, 0.0).astype(bf16))
        tot = mm_nt(beside(*left), beside(*right))
        return [
            tot[c * wrow : (c + 1) * wrow] + tot[(3 + c) * wrow : (4 + c) * wrow] for c in range(3)
        ]

    def scatter_steps(group):
        for s in range(group * 4, group * 4 + 4):
            at = lambda l: slice(s * blocks + l, s * blocks + l + 1)
            parts = vertex_sums(lambda l: [grad[c, at(l), :] for c in range(6)], at)
            r = s % 4
            for c in range(3):
                if r in (1, 2):
                    acc[c][group] = acc[c][group] + parts[c]
                else:
                    edge, to = (3, (group - 1) % groups) if r == 0 else (0, (group + 1) % groups)
                    acc[c][to] = acc[c][to] + jnp.where(rmod == edge, parts[c], 0.0)
                    acc[c][group] = acc[c][group] + jnp.where(rmod == edge, 0.0, parts[c])
            yield

    for group in range(groups):
        behind = scatter_steps(group - 1) if group else iter(())
        for step, _ in enumerate(far_steps(group)):
            next(near_steps, None)
            if step % 2 == 0:
                next(behind, None)
        for _ in behind:
            pass
    for _ in near_steps:
        pass
    for _ in scatter_steps(groups - 1):
        pass

    def near_values(l):
        fi, di, xi = mine_of[l][:3]
        o = hold["o", l]
        o = o[0:8] + o[8:16]
        values = [
            scale * (di * (o[c : c + 1] - xi[c] * o[3:4]) + fi * (o[4 + c : 5 + c] - xi[c] * o[7:8]))
            for c in range(3)
        ]
        highs = [v.astype(bf16).astype(f32) for v in values]
        return highs + [v - h for v, h in zip(values, highs)]

    parts = vertex_sums(near_values, lambda l: pl.ds(base + l, 1))
    for side in range(-1, 2):
        owner = (slab + side + slabs) % slabs
        for group in range(groups):
            mine = (rmod == owner % 4) & (owner // 4 == group)
            for c in range(3):
                acc[c][group] = acc[c][group] + jnp.where(mine, parts[c], 0.0)
    zero = jnp.zeros((wrow, 128 - 3 * VCH), f32)
    for q in range(groups):
        rows = beside(acc[0][q], acc[1][q], acc[2][q], zero)
        for e in range(exc):
            out[e * slabs + 4 * q : e * slabs + 4 * q + 4, :] = rows[4 * e : 4 * e + 4]


def sum_kernel(parts, out):
    row = jnp.sum(parts[...], axis=0, keepdims=True)
    for c in range(3):
        out[c : c + 1, :] = row[:, c * VCH : (c + 1) * VCH]


def on_device(
    q_forward, q_adjoint, panel_offset, block_anchor, kernel_hat, near_list, near_count,
    panel_vertices,
):
    slabs, exc = lax.axis_size("slab"), lax.axis_size("exc")
    blocks = block_anchor.shape[1]
    g, thick = kernel_hat.shape[0], kernel_hat.shape[1]
    nblk = slabs * blocks
    shape = lambda *s, t=f32: jax.ShapeDtypeStruct(s, t)
    params = pltpu.CompilerParams(vmem_limit_bytes=LIMIT)
    rows = QROWS * blocks
    packed = pl.pallas_call(
        functools.partial(pack_kernel, slabs, blocks),
        out_shape=shape(slabs, 5, blocks, 128),
        in_specs=[VM, VM, VM, SM, VM],
        out_specs=VM,
        scratch_shapes=[pltpu.VMEM((rows, 128), f32)],
        name="pack",
    )(q_forward, q_adjoint, panel_offset, block_anchor, panel_vertices)
    consts, prep_consts, lanes = tables(g, thick)
    lanes = jnp.asarray(lanes)
    facts = jnp.concatenate([near_count, near_list.reshape(-1)])
    ready = pl.pallas_call(
        functools.partial(prep_kernel, thick),
        out_shape=(
            shape(thick, g, g), shape(thick, g // 2, g),
            shape(384, 256, t=bf16), shape(256, 128, t=bf16), shape(g, 512, t=bf16),
        ),
        in_specs=[VM] * 4,
        out_specs=(VM,) * 5,
        compiler_params=params,
        name="prep",
    )(kernel_hat, *[jnp.asarray(c) for c in prep_consts], lanes)
    gathered = lax.all_to_all(packed, "slab", split_axis=0, concat_axis=0, tiled=True)
    swapped = lax.ppermute(gathered, "slab", [(i, i ^ 1) for i in range(slabs)])
    coef = pl.pallas_call(
        functools.partial(spectrum_kernel, slabs, blocks, thick, g),
        out_shape=shape(3 * nblk, 128),
        in_specs=[VM] * (7 + len(consts)),
        out_specs=VM,
        scratch_shapes=[
            pltpu.VMEM((nblk, 128), f32),
            pltpu.VMEM((thick * 3 * nblk, 2 * g), f32),
        ],
        compiler_params=params,
        cost_estimate=pl.CostEstimate(flops=10**9, bytes_accessed=2 * 10**6, transcendentals=0),
        name="spectrum",
    )(gathered, *ready, *[jnp.asarray(c) for c in consts], lanes)
    partial = pl.pallas_call(
        functools.partial(panel_kernel, slabs, exc, blocks, near_list.shape[1]),
        out_shape=shape(exc * slabs, 128),
        in_specs=[pl.BlockSpec(memory_space=pl.ANY)] + [VM] * 3,
        out_specs=VM,
        scratch_shapes=[
            pltpu.VMEM((QROWS, nblk, 128), f32),
            pltpu.VMEM((6, nblk, 128), f32),
            pltpu.VMEM((6, nblk, 128), f32),
            pltpu.SMEM(facts.shape, jnp.int32),
            pltpu.SemaphoreType.DMA,
        ],
        compiler_params=params,
        name="panel",
    )(facts, gathered, swapped, coef)
    parts = lax.all_to_all(partial, ("exc", "slab"), split_axis=0, concat_axis=0, tiled=True)
    return pl.pallas_call(
        sum_kernel, out_shape=shape(3, VCH), in_specs=[VM], out_specs=VM,
        compiler_params=params, name="total",
    )(parts)


def solution(mesh):
    return jax.shard_map(
        on_device,
        mesh=mesh,
        in_specs=(
            P("exc", "slab"),
            P("exc", "slab"),
            P(None, "slab"),
            P(None, "slab"),
            P(None, "slab", None),
            P("slab", None),
            P("slab"),
            P(None, "slab"),
        ),
        out_specs=P(None, ("exc", "slab")),
        check_vma=False,
    )
```

```python
import functools
import math

import jax
import jax.numpy as jnp
import numpy as np
from jax import lax
from jax.experimental import pallas as pl
from jax.experimental.pallas import tpu as pltpu
from jax.sharding import PartitionSpec as P

VCH = 32
QROWS = 9
soften_sq = 16.0
bf16 = jnp.bfloat16
f32 = jnp.float32
VM = pl.BlockSpec(memory_space=pltpu.VMEM)
SM = pl.BlockSpec(memory_space=pltpu.SMEM)
LIMIT = 24 << 20
PACE = 0
FLAGS = None


def split(x):
    high = x.astype(bf16)
    return high, (x - high.astype(f32)).astype(bf16)


def mm(a, b):
    return lax.dot_general(a, b, (((1,), (0,)), ((), ())), preferred_element_type=f32)


def mm_nt(a, b):
    return lax.dot_general(a, b, (((1,), (1,)), ((), ())), preferred_element_type=f32)


def beside(*parts):
    return jnp.concatenate(parts, axis=1)


def below(*parts):
    return jnp.concatenate(parts, axis=0)


def iota(shape, dim):
    return lax.broadcasted_iota(jnp.int32, shape, dim)


def columns(thick):
    lane = iota((1, 128), 1) & 63
    lane_in = jnp.where(lane >= 3 * thick, lane - 3 * thick, lane).astype(f32)
    return jnp.where(lane < 6 * thick, jnp.floor((lane_in + 0.5) * (1.0 / 3.0)), -1.0).astype(jnp.int32)


@functools.lru_cache(None)
def tables(g, thick):
    n = np.arange(g)
    ang = 2.0 * np.pi * (np.outer(n, n) % g) / g
    cos, sin = np.cos(ang), np.sin(ang)
    th = 2.0 * np.pi * n / g
    u = np.stack([np.ones(g), -1j * np.sin(th), np.cos(th) - 1.0])
    half = g // 2
    e = u[:, :, None] * (cos - 1j * sin)[None]
    rows = np.concatenate([e.real[:, : half + 1], -e.imag[:, 1:half]], axis=1)
    ct = np.concatenate([rows[k].T for k in range(3)], axis=1)
    cz = np.concatenate([cos, sin], axis=1)
    nb3 = 3 * thick
    up = np.zeros((64, 2 * g))
    dn = np.zeros((2 * g, 64))
    m = np.zeros((2, 3, 128, 64))
    bt = np.zeros((2, 3, 64, 128))
    for b in range(thick):
        for k in range(3):
            r, i = b * 3 + k, nb3 + b * 3 + k
            up[r, :g], up[r, g:] = u[k].real, u[k].imag
            up[i, :g], up[i, g:] = -u[k].imag, u[k].real
            uc = np.conj(u[k])
            dn[:g, r], dn[g:, r] = uc.real, -uc.imag
            dn[:g, i], dn[g:, i] = uc.imag, uc.real
            for al in range(3):
                f0, f1 = al * 9 + k, 27 + al * 9 + k
                m[0, 0, f0, r] = 1
                m[0, 0, f1, i] = 1
                m[0, 1, f0 + 3, i] = -1
                m[0, 1, f1 + 3, r] = 1
                m[0, 2, f0 + 6, r] = 1
                m[0, 2, f1 + 6, i] = 1
            bt[0, 0, r, k] = 1
            bt[0, 0, i, 9 + k] = 1
            bt[0, 1, r, 9 + 3 + k] = 1
            bt[0, 1, i, 3 + k] = -1
            bt[0, 2, r, 6 + k] = 1
            bt[0, 2, i, 9 + 6 + k] = 1
    bt[..., 64:] = bt[..., :64]
    real, imag = slice(0, nb3), slice(nb3, 2 * nb3)
    m[1, ..., real], m[1, ..., imag] = m[0, ..., imag], -m[0, ..., real]
    bt[1, :, real], bt[1, :, imag] = bt[0, :, imag], -bt[0, :, real]
    bt = bt / float(g) ** 3
    m = np.concatenate([m, m], axis=3)
    def halves(x):
        high = x.astype(np.float32).astype(bf16)
        return high, (x.astype(np.float32) - high.astype(np.float32)).astype(bf16)

    ct_h, ct_l = halves(ct)
    cz_h, cz_l = halves(cz)
    up_h, up_l = halves(up)
    dn_h, dn_l = halves(dn)
    up4 = np.concatenate([up_h, up_h, up_l, np.zeros_like(up_l)], axis=0)
    dn2 = np.concatenate([dn_h, dn_l], axis=1)
    ctz = np.concatenate([ct_h, ct_l], axis=1)
    czz = np.concatenate([cz_h, cz_l], axis=1)
    return (ctz, czz, up4, dn2), (m[:, :, :64].astype(bf16), bt.astype(bf16))


def pack_kernel(slabs, blocks, qf, qa, off, anchor, verts, out, buf):
    width = qf.shape[1] // blocks
    buf[...] = jnp.zeros_like(buf)
    for l in range(blocks):
        cut = slice(l * width, (l + 1) * width)
        buf[blocks + l : blocks + l + 1, :] = qf[:, cut]
        buf[2 * blocks + l : 2 * blocks + l + 1, :] = qa[:, cut]
        for c in range(3):
            row = (3 + c) * blocks + l
            buf[row : row + 1, :] = off[c : c + 1, cut]
            row = (6 + c) * blocks + l
            buf[row : row + 1, :] = verts[c : c + 1, cut].astype(f32)
    part = lambda q: buf[q * blocks : (q + 1) * blocks, :]
    t0, t1, t2 = part(3), part(4), part(5)
    lane = iota((blocks, 128), 1)
    sub = iota((blocks, 128), 0)
    odd = sub % 2 * 64
    acc = jnp.zeros((blocks, 128), f32)
    for f in range(2):
        x = part(1 + f)
        for al in range(3):
            y = x
            for be in range(3):
                z = y
                for ga in range(3):
                    idx = f * 27 + al * 9 + be * 3 + ga
                    acc = jnp.where(lane == idx + odd, jnp.sum(z, axis=1, keepdims=True), acc)
                    z = z * t2
                y = y * t1
            x = x * t0
    for l in range(blocks):
        for c in range(3):
            hit = (lane == 54 + c + odd) & (sub == l)
            acc = jnp.where(hit, anchor[c, l].astype(f32), acc)
    buf[0:blocks, :] = acc
    head = below(*[buf[l : l + 1, :] + buf[l + 1 : l + 2, :] for l in range(0, blocks, 2)])
    pairs = blocks // 2
    pieces = [buf[l : l + pairs, :] for l in range(blocks, QROWS * blocks, pairs)]
    for j in range(slabs):
        out[j, 0] = head
        for k in range(8):
            out[j, 1 + k] = pieces[j % 2 * 8 + k]


def prep_kernel(thick, k, m_t, bt_t, ka, kd, mo, bo, fy):
    g = k.shape[0]
    half = g // 2
    for a in range(half):
        if a == 0:
            top, bot, dif = k[0], k[half], jnp.zeros_like(k[0])
        else:
            top = k[a] + k[g - a]
            bot, dif = top, k[a] - k[g - a]
        ka[:, a, :] = top
        ka[:, half + a, :] = bot
        kd[:, a, :] = dif
    freq = columns(thick) + lax.axis_index("slab") * thick
    step = 2.0 * math.pi / g
    th = freq.astype(f32) * step
    sn, cm = jnp.sin(th), jnp.cos(th) - 1.0
    wide = lambda t, v, x: t[v, 0].astype(f32) + t[v, 1].astype(f32) * x[0] + t[v, 2].astype(f32) * x[1]
    forms = [wide(m_t, v, (sn, cm)) for v in range(2)]
    h, l = split(below(beside(*forms), jnp.zeros((64, 256), f32)))
    mo[...] = below(h, h, l)
    down = lambda row: jnp.transpose(jnp.broadcast_to(row, (128, 128)))[:64]
    sn, cm = down(sn), down(cm)
    back = [wide(bt_t, v, (sn, cm)) for v in (0, 0, 1, 1)]
    h, l = split(below(*back))
    bo[...] = jnp.where(iota(h.shape, 1) < 64, h.astype(f32), l.astype(f32)).astype(bf16)
    turn = ((iota((g, 128), 0) * freq) & (g - 1)).astype(f32) * step
    ch, cl = split(jnp.cos(turn))
    sh, sl = split(jnp.sin(turn))
    fy[...] = beside(ch, sh, cl, sl)


def stagger(count, *stages):
    for step in range(count + len(stages) - 1):
        for k, stage in enumerate(stages):
            if 0 <= step - k < count:
                stage(step - k)
        yield


def spectrum_kernel(
    slabs, blocks, thick, g,
    gat, ka, kd, mo, bo, fy, ct_t, cz_t, up_t, dn_t,
    out, head_ref, kept, expand,
):
    nblk = slabs * blocks
    half = g // 2
    pairs = blocks // 2
    for s in range(slabs):
        both = gat[s, 0]
        for l in range(blocks):
            head_ref[s * blocks + l : s * blocks + l + 1, :] = both[l // 2 : l // 2 + 1]
        for k in range(8):
            at = s * blocks + k % 2 * pairs
            kept[k // 2, at : at + pairs, :] = gat[s, 1 + k]
    head = head_ref[...]
    head = jnp.where(iota(head.shape, 0) % 2 == 1, pltpu.roll(head, 64, 1), head)
    head_ref[...] = head
    lane = iota((nblk, 128), 1)
    glane = iota((nblk, g), 1).astype(f32)
    hot = lambda c: jnp.where(glane == head[:, 54 + c : 55 + c], 1.0, 0.0).astype(bf16)
    ph = mm(hot(1), fy[...])
    ph = ph[:, :256] + ph[:, 256:]
    pc, ps = ph[:, :128], ph[:, 128:]
    qs = []
    for al in range(3):
        lo, hi = al * 9, al * 9 + 9
        keep = ((lane >= lo) & (lane < hi)) | ((lane >= 27 + lo) & (lane < 27 + hi))
        h, l = split(jnp.where(keep, head, 0.0))
        qs.append(beside(h, l, h))
    v = mm(below(*qs), mo[...])
    v = v[:, :128] * below(pc, pc, pc) + v[:, 128:] * below(ps, ps, ps)
    vh = v.astype(bf16).astype(f32)
    v = jnp.where(iota(v.shape, 1) < 64, vh, v - vh)
    vlane = columns(thick)
    m3 = 3 * nblk
    vb = below(*[jnp.where(vlane == b, v, 0.0) for b in range(thick)]).astype(bf16)
    expand[...] = mm(beside(vb, vb), up_t[...])
    cth = mm(hot(0), ct_t[...])
    rows3 = lambda x, o: below(*[x[:, o + k * g : o + (k + 1) * g] for k in range(3)])
    ct_h, ct_l = rows3(cth, 0), rows3(cth, 3 * g)
    cc_h = jnp.transpose(ct_h).astype(bf16)
    cc = below(cc_h, jnp.transpose(ct_l).astype(bf16))
    ct_h, ct_l = ct_h.astype(bf16), ct_l.astype(bf16)
    ct = below(beside(ct_h, ct_h), beside(ct_l, jnp.zeros_like(ct_l)))
    wz = mm(hot(2), cz_t[...])
    wz = wz[:, : 2 * g] + wz[:, 2 * g :]
    wc = below(*[wz[:, :g]] * 3)
    ws = below(*[wz[:, g:]] * 3)
    hold = {"x": jnp.zeros(v.shape, f32)}

    def forward(b):
        ar, ai = expand[b * m3 : (b + 1) * m3, :g], expand[b * m3 : (b + 1) * m3, g:]
        rh, rl = split(beside(ar * wc + ai * ws, ai * wc - ar * ws))
        pn = mm(cc, rh)
        hold["pn", b] = pn[:g] + pn[g:] + mm(cc_h, rl)

    def backward(b):
        pn = hold.pop(("pn", b))
        pr, pi = pn[:half, :g], pn[:half, g:]
        nr, ni = pn[half:, :g], pn[half:, g:]
        kt, kb, kx = ka[b, :half, :], ka[b, half:, :], kd[b]
        top = beside(pr * kt + ni * kx, pi * kt - nr * kx)
        bot = beside(nr * kb - pi * kx, ni * kb + pr * kx)
        th, tl = split(below(top, bot))
        z = mm(ct, below(th, tl))
        hold["z", b] = z[:m3] + z[m3:]

    def reduce(b):
        z = hold.pop(("z", b))
        zr, zi = z[:, :g], z[:, g:]
        hold["y", b] = split(beside(zr * wc - zi * ws, zi * wc + zr * ws))
        if b % 2 or b == thick - 1:
            both = [hold.pop(("y", k)) for k in range(b - b % 2, b + 1)]
            xs = mm(below(*[half for y in both for half in y]), dn_t[...])
            for k in range(len(both)):
                sums = xs[2 * k * m3 : (2 * k + 1) * m3] + xs[(2 * k + 1) * m3 : (2 * k + 2) * m3]
                hold["x"] = jnp.where(vlane == b - b % 2 + k, sums, hold["x"])

    for _ in stagger(thick, forward, backward, reduce):
        pass
    x = hold["x"]
    h, l = split(beside(x * below(pc, pc, pc), x * below(ps, ps, ps)))
    coef = mm(below(h, l), bo[...])
    coef = coef[:m3] + coef[m3:]
    out[...] = coef + pltpu.roll(coef, 64, 1)


def panel_kernel(
    slabs, exc, blocks, slots,
    facts, head, kept, swapped, coef,
    out, qs, verts, grad, rows_ref,
):
    nblk = slabs * blocks
    slab = lax.axis_index("slab")
    qs[0] = head[...]
    parity = slab % 2
    pairs = blocks // 2
    for q in range(4):
        qs[1 + q + 4 * parity] = kept[q]
    for s in range(slabs):
        for k in range(8):
            at = s * blocks + k % 2 * pairs
            qs[5 + k // 2 - 4 * parity, at : at + pairs, :] = swapped[s, 1 + k]
    base = slab * blocks
    sub8 = iota((8, 128), 0)
    scale = 1.0 / (3.0 * exc)
    pairs = slots // 2
    hold, mine_of = {}, {}
    lane = iota((blocks * slots, 2 * nblk), 1).astype(f32)
    count = blocks * slots
    known = beside(facts[...].astype(f32), jnp.zeros((1, 128 - count - blocks), f32))
    column = jnp.transpose(jnp.broadcast_to(known, (128, 128)))[:, 0:1]
    slot_of = iota((slots, 1), 0).astype(f32)
    ids = below(*[
        jnp.where(slot_of < column[count + l : count + l + 1], column[l * slots : (l + 1) * slots], -4.0 * nblk)
        for l in range(blocks)
    ])
    pick = (lane == ids) | (lane == ids + float(nblk))
    halves = [split(qs[q]) for q in range(6)]
    data = below(beside(*[h for h, _ in halves]), beside(*[l for _, l in halves]))
    near_data = mm(jnp.where(pick, 1.0, 0.0).astype(bf16), data)

    def near_rows(l):
        own = lambda q: qs[q, pl.ds(base + l, 1), :]
        fi, di, xi, me = own(1), own(2), [own(3 + c) for c in range(3)], own(0)
        size = xi[0] * xi[0] + xi[1] * xi[1] + xi[2] * xi[2] + soften_sq
        mine = jnp.where(sub8 == 3, 1.0, jnp.where(sub8 == 4, size, 0.0))
        for c in range(3):
            mine = jnp.where(sub8 == c, xi[c], mine)
        mh = mine.astype(bf16).astype(f32)
        left = jnp.transpose(below(mh, mh, mine - mh, jnp.zeros((104, 128), f32)))
        mine_of[l] = (fi, di, xi, left[:, :32].astype(bf16))
        hold["o", l] = jnp.zeros((16, 128), f32)
        part = lambda q: near_data[l * slots : (l + 1) * slots, q * 128 : (q + 1) * 128]
        away = part(0)
        xr = [part(3 + c) + (away[:, 54 + c : 55 + c] - me[:, 54 + c : 55 + c]) for c in range(3)]
        sq = xr[0] * xr[0] + xr[1] * xr[1] + xr[2] * xr[2]
        one, zero = jnp.ones_like(sq), jnp.zeros_like(sq)
        weighted = [part(1) * x for x in xr + [one]] + [part(2) * x for x in xr + [one]]
        start = l * 32 * slots
        for which, items in enumerate(([-2.0 * x for x in xr] + [sq, one, zero, zero, zero], weighted)):
            for k, item in enumerate(items):
                high = item.astype(bf16).astype(f32)
                at = start + (which * 16 + k) * slots
                rows_ref[at : at + slots, :] = high
                rows_ref[at + 8 * slots : at + 9 * slots, :] = item - high

    def gather_pair(n):
        l, first = n // pairs, n % pairs * 2
        if first == 0:
            near_rows(l)
        right, sums = [], []
        for slot in range(first, min(first + 2, slots)):
            take = lambda k: rows_ref[pl.ds(l * 32 * slots + 8 * k * slots + slot, 8, stride=slots), :]
            high, low = take(0), take(1)
            right.append(below(high, low, high, jnp.zeros((8, 128), f32)).astype(bf16))
            sums.append(below(take(2), take(3)).astype(bf16))
        hold["right", n] = beside(*right)
        hold["sums", n] = beside(*sums, *sums)

    def distance_pair(n):
        hold["d", n] = mm(mine_of[n // pairs][3], hold.pop(("right", n)))

    def cube_pair(n):
        inv = lax.rsqrt(hold.pop(("d", n)))
        hold["cube", n] = beside(*split(inv * inv * inv))

    def sum_pair(n):
        l = n // pairs
        hold["o", l] = hold["o", l] + mm_nt(hold.pop(("sums", n)), hold.pop(("cube", n)))

    near_steps = stagger(blocks * pairs, gather_pair, distance_pair, cube_pair, sum_pair)
    wrow = 4 * exc
    hrow = iota((wrow, 128), 0).astype(f32)
    lrow = iota((VCH, 128), 0).astype(f32)
    rmod = iota((wrow, VCH), 0) % 4
    groups = slabs // 4
    acc = [[jnp.zeros((wrow, VCH), f32) for _ in range(groups)] for _ in range(3)]

    def far_steps(group):
        to = slice(group * 4 * blocks, (group + 1) * 4 * blocks)
        qf, qa, t0, t1, t2 = (qs[k, to, :] for k in range(1, 6))
        va, vb, vc = [], [], []
        for al in range(3):
            rows = coef[al * nblk + to.start : al * nblk + to.stop, :]
            mid = []
            for be in range(3):
                h = []
                for ga in range(3):
                    k = be * 3 + ga
                    h.append(qa * rows[:, k : k + 1] + qf * rows[:, 9 + k : 10 + k])
                d2 = t2 * h[2]
                e2 = h[1] + d2
                mid.append((h[0] + t2 * e2, e2 + d2))
                yield
            d1 = t1 * mid[2][0]
            e1 = mid[1][0] + d1
            va.append(mid[0][0] + t1 * e1)
            vb.append(e1 + d1)
            vc.append(mid[0][1] + t1 * (mid[1][1] + t1 * mid[2][1]))
        total = (
            va[1] + 2.0 * t0 * va[2],
            vb[0] + t0 * (vb[1] + t0 * vb[2]),
            vc[0] + t0 * (vc[1] + t0 * vc[2]),
        )
        for c in range(3):
            value = total[c] * scale
            high = value.astype(bf16).astype(f32)
            grad[c, to, :] = high
            grad[3 + c, to, :] = value - high
        for k in range(3):
            vert = qs[6 + k, to, :]
            chunk = jnp.floor((vert + 0.5) * (1.0 / VCH))
            part = jnp.floor((chunk + 0.5) * (1.0 / slabs))
            verts[k, to, :] = 4.0 * part + (chunk - 4.0 * jnp.floor(chunk * 0.25))
            verts[3 + k, to, :] = vert - float(VCH) * chunk

    def vertex_sums(values_of, row_of):
        left, right = [], []
        for l in range(blocks):
            values, row = values_of(l), row_of(l)
            for k in range(3):
                hit = hrow == verts[k, row, :]
                left.append(below(*[jnp.where(hit, p, 0.0) for p in values]).astype(bf16))
                right.append(jnp.where(lrow == verts[3 + k, row, :], 1.0, 0.0).astype(bf16))
        tot = mm_nt(beside(*left), beside(*right))
        return [
            tot[c * wrow : (c + 1) * wrow] + tot[(3 + c) * wrow : (4 + c) * wrow] for c in range(3)
        ]

    def scatter_steps(group):
        for s in range(group * 4, group * 4 + 4):
            at = lambda l: slice(s * blocks + l, s * blocks + l + 1)
            parts = vertex_sums(lambda l: [grad[c, at(l), :] for c in range(6)], at)
            r = s % 4
            for c in range(3):
                if r in (1, 2):
                    acc[c][group] = acc[c][group] + parts[c]
                else:
                    edge, to = (3, (group - 1) % groups) if r == 0 else (0, (group + 1) % groups)
                    acc[c][to] = acc[c][to] + jnp.where(rmod == edge, parts[c], 0.0)
                    acc[c][group] = acc[c][group] + jnp.where(rmod == edge, 0.0, parts[c])
            yield

    for group in range(groups):
        behind = scatter_steps(group - 1) if group else iter(())
        for step, _ in enumerate(far_steps(group)):
            if group * 9 + step >= PACE:
                next(near_steps, None)
            if step % 2 == 0:
                next(behind, None)
        for _ in behind:
            pass
    for _ in near_steps:
        pass
    for _ in scatter_steps(groups - 1):
        pass

    def near_values(l):
        fi, di, xi = mine_of[l][:3]
        o = hold["o", l]
        o = o[0:8] + o[8:16]
        values = [
            scale * (di * (o[c : c + 1] - xi[c] * o[3:4]) + fi * (o[4 + c : 5 + c] - xi[c] * o[7:8]))
            for c in range(3)
        ]
        highs = [v.astype(bf16).astype(f32) for v in values]
        return highs + [v - h for v, h in zip(values, highs)]

    parts = vertex_sums(near_values, lambda l: pl.ds(base + l, 1))
    for side in range(-1, 2):
        owner = (slab + side + slabs) % slabs
        for group in range(groups):
            mine = (rmod == owner % 4) & (owner // 4 == group)
            for c in range(3):
                acc[c][group] = acc[c][group] + jnp.where(mine, parts[c], 0.0)
    zero = jnp.zeros((wrow, 128 - 3 * VCH), f32)
    for q in range(groups):
        rows = beside(acc[0][q], acc[1][q], acc[2][q], zero)
        for e in range(exc):
            out[e * slabs + 4 * q : e * slabs + 4 * q + 4, :] = rows[4 * e : 4 * e + 4]


def sum_kernel(parts, out):
    row = jnp.sum(parts[...], axis=0, keepdims=True)
    for c in range(3):
        out[c : c + 1, :] = row[:, c * VCH : (c + 1) * VCH]


def on_device(
    q_forward, q_adjoint, panel_offset, block_anchor, kernel_hat, near_list, near_count,
    panel_vertices,
):
    slabs, exc = lax.axis_size("slab"), lax.axis_size("exc")
    blocks = block_anchor.shape[1]
    g, thick = kernel_hat.shape[0], kernel_hat.shape[1]
    nblk = slabs * blocks
    shape = lambda *s, t=f32: jax.ShapeDtypeStruct(s, t)
    params = pltpu.CompilerParams(vmem_limit_bytes=LIMIT)
    tuned = pltpu.CompilerParams(vmem_limit_bytes=LIMIT, flags=FLAGS)
    rows = QROWS * blocks
    packed = pl.pallas_call(
        functools.partial(pack_kernel, slabs, blocks),
        out_shape=shape(slabs, 9, blocks // 2, 128),
        in_specs=[VM, VM, VM, SM, VM],
        out_specs=VM,
        scratch_shapes=[pltpu.VMEM((rows, 128), f32)],
        name="pack",
    )(q_forward, q_adjoint, panel_offset, block_anchor, panel_vertices)
    consts, prep_consts = tables(g, thick)
    slots = near_list.shape[1]
    facts = jnp.concatenate([near_list.reshape(-1), near_count]).reshape(1, -1)
    ready = pl.pallas_call(
        functools.partial(prep_kernel, thick),
        out_shape=(
            shape(thick, g, g), shape(thick, g // 2, g),
            shape(384, 256, t=bf16), shape(256, 128, t=bf16), shape(g, 512, t=bf16),
        ),
        in_specs=[VM] * 3,
        out_specs=(VM,) * 5,
        compiler_params=params,
        cost_estimate=pl.CostEstimate(flops=10**9, bytes_accessed=2 * 10**6, transcendentals=0),
        name="prep",
    )(kernel_hat, *[jnp.asarray(c) for c in prep_consts])
    gathered = lax.all_to_all(packed, "slab", split_axis=0, concat_axis=0, tiled=True)
    gathered, ready, facts = lax.optimization_barrier((gathered, ready, facts))
    swapped = lax.ppermute(gathered, "slab", [(i, i ^ 1) for i in range(slabs)])
    coef, head, kept = pl.pallas_call(
        functools.partial(spectrum_kernel, slabs, blocks, thick, g),
        out_shape=(shape(3 * nblk, 128), shape(nblk, 128), shape(4, nblk, 128)),
        in_specs=[VM] * (6 + len(consts)),
        out_specs=(VM,) * 3,
        scratch_shapes=[
            pltpu.VMEM((thick * 3 * nblk, 2 * g), f32),
        ],
        compiler_params=tuned,
        cost_estimate=pl.CostEstimate(flops=10**9, bytes_accessed=2 * 10**6, transcendentals=0),
        name="spectrum",
    )(gathered, *ready, *[jnp.asarray(c) for c in consts])
    partial = pl.pallas_call(
        functools.partial(panel_kernel, slabs, exc, blocks, slots),
        out_shape=shape(exc * slabs, 128),
        in_specs=[VM] * 5,
        out_specs=VM,
        scratch_shapes=[
            pltpu.VMEM((QROWS, nblk, 128), f32),
            pltpu.VMEM((6, nblk, 128), f32),
            pltpu.VMEM((6, nblk, 128), f32),
            pltpu.VMEM((32 * blocks * slots, 128), f32),
        ],
        compiler_params=tuned,
        name="panel",
    )(facts, head, kept, swapped, coef)
    parts = lax.all_to_all(partial, ("exc", "slab"), split_axis=0, concat_axis=0, tiled=True)
    return pl.pallas_call(
        sum_kernel, out_shape=shape(3, VCH), in_specs=[VM], out_specs=VM,
        compiler_params=params, name="total",
    )(parts)


def solution(mesh):
    return jax.shard_map(
        on_device,
        mesh=mesh,
        in_specs=(
            P("exc", "slab"),
            P("exc", "slab"),
            P(None, "slab"),
            P(None, "slab"),
            P(None, "slab", None),
            P("slab", None),
            P("slab"),
            P(None, "slab"),
        ),
        out_specs=P(None, ("exc", "slab")),
        check_vma=False,
    )
```
